32 devices in a mesh: groups: 2 (over y), gz: 4 (over z), xy: 2 (over x), col: 2 (over core).
Axes of the slice: x: 2, y: 2, z: 4, core: 2. Of those that a mesh axis runs over, the one named last changes fastest.
Arguments:
- features: bfloat16 [8, 16, 256, 256], P(('groups', 'gz'), None, ('xy', 'col')), parts along dimension 0, may hold values from -24 to 24
- class_map: int32 [8, 256, 256], P(('groups', 'gz'), ('xy', 'col')), parts along dimension 0, may hold values from 0 to 3
- stiffness: float32 [4], replicated, may hold values from 0.2 to 2
- valid: int32 [8, 4], P('groups'), parts along dimension 0, may hold values 0 or 1
Outputs:
- displacement: float32 [8, 2, 256, 256], P(('groups', 'gz'), None, ('xy', 'col')), parts along dimension 0
- forward_flow: float32 [8, 2, 256, 256], P(('groups', 'gz'), None, ('xy', 'col')), parts along dimension 0
The draws below stay inside these ranges and needn't reach their ends.
There are 2 independent parts, one for each index of `groups`. The reference program is written for one: setup_inputs(seed, part) draws one part's arguments, and reference() takes and returns one part's arrays. A program takes and returns all parts, laid end to end along the dimension named above; an argument that names none is the same for every part. Nothing has to cross between parts.
All inputs are finite; a program needn't handle non-finite values.
Results may differ from the reference program's by a relative error of at most 0.0017.
Values may be sent and summed in bfloat16 or wider, within the bound.
No kernel may reach another device: no remote copies, remote signals or barrier semaphores. Data moves between devices by JAX's collectives and lax.ppermute only.
A program may use at most 64 MiB of HBM per device.

```python
import math
import jax
import jax.numpy as jnp
from jax import lax

CHANNELS = 16
RADIUS = 6
CLASSES = 4
STEPS = 3
TILE_ROWS = 64
TILE_COLS = 256
TILES = 4
SECTIONS = 4
SECT_ROWS = 256


def draw_features(key, part):
    shape = (SECTIONS, CHANNELS, SECT_ROWS, TILE_COLS)
    values = jnp.clip(jax.random.normal(key, shape, jnp.float32), -4.0, 4.0)
    return values.astype(jnp.bfloat16)


def with_ends(entries, stream_key, low, top_value):
    longest = entries.shape.index(max(entries.shape))
    spots = []
    for shift in (0, 1):
        where = [jax.random.randint(jax.random.fold_in(stream_key, axis), (), 0, length) for axis, length in enumerate(entries.shape)]
        where[longest] = (where[longest] + shift) % entries.shape[longest]
        spots.append(tuple(where))
    return entries.at[spots[0]].set(low).at[spots[1]].set(top_value)


def setup_inputs(seed: int = 0, part: int = 0) -> dict:
    splits = jax.random.split(jax.random.key(seed), 5)
    own_keys = jax.random.split(jax.random.fold_in(splits[4], part), 5)
    return {
        "features": draw_features(jax.random.fold_in(jax.random.fold_in(splits[4], part), 71), part),
        "class_map": with_ends(jax.random.randint(own_keys[1], (SECTIONS, SECT_ROWS, TILE_COLS), 0, CLASSES), jax.random.fold_in(own_keys[1], 1), 0, CLASSES - 1).astype(jnp.int32),
        "stiffness": jnp.clip(jnp.exp(jax.random.uniform(splits[2], (CLASSES,), jnp.float32, math.log(0.2), math.log(2.0))), 0.2, 2.0),
        "valid": with_ends((jax.random.randint(own_keys[3], (SECTIONS, TILES), 0, 4) < 3).astype(jnp.int32), jax.random.fold_in(own_keys[3], 1), 0, 1),
    }


score_scale = 0.25
step_size = 0.1
saturation = 2.0

def expected(stacked):
    highest = lax.optimization_barrier(jnp.max(stacked, axis=0))
    weights = jnp.exp(stacked - highest)
    denominator = lax.optimization_barrier(jnp.sum(weights, axis=0))
    window = 2 * RADIUS + 1
    places = jnp.arange(window * window, dtype=jnp.int32)
    row_shift = (places // window - RADIUS).astype(jnp.float32)
    col_shift = (places % window - RADIUS).astype(jnp.float32)
    flow_row = lax.optimization_barrier(jnp.sum(weights * row_shift[:, None, None], axis=0)) / denominator
    flow_col = lax.optimization_barrier(jnp.sum(weights * col_shift[:, None, None], axis=0)) / denominator
    return jnp.stack([flow_row, flow_col])

def band_scores(center_band, window_band, height, breadth):
    scores = []
    for shift_row in range(2 * RADIUS + 1):
        for shift_col in range(2 * RADIUS + 1):
            scores.append(lax.optimization_barrier(jnp.sum(center_band * window_band[:, shift_row:shift_row + height, shift_col:shift_col + breadth], axis=0)))
    return score_scale * jnp.stack(scores)

def elastic_term(disp_pad, stiff_pad):
    middle = disp_pad[..., 1:-1, 1:-1]
    stiff_mid = stiff_pad[..., 1:-1, 1:-1]
    result = jnp.zeros_like(middle)
    for row_part, col_part in ((slice(2, None), slice(1, -1)), (slice(0, -2), slice(1, -1)), (slice(1, -1), slice(2, None)), (slice(1, -1), slice(0, -2))):
        neighbour_stiff = stiff_pad[..., row_part, col_part]
        result = result + 0.5 * (stiff_mid + neighbour_stiff) * (middle - disp_pad[..., row_part, col_part])
    return result

def spring(vector):
    return vector / jnp.sqrt(1.0 + lax.optimization_barrier(jnp.sum(vector * vector, axis=-3, keepdims=True)) / (saturation * saturation))

def section_flow(pair_items):
    center, other = pair_items
    padded = jnp.pad(other, ((0, 0), (RADIUS, RADIUS), (RADIUS, RADIUS)))
    height, breadth = (center.shape[1], center.shape[2])
    return expected(band_scores(center.astype(jnp.float32), padded.astype(jnp.float32), height, breadth))

def reference(features, class_map, stiffness, valid):
    blank = jnp.zeros_like(features[:1])
    nexts = jnp.concatenate([features[1:], blank], axis=0)
    priors = jnp.concatenate([blank, features[:-1]], axis=0)
    forward = lax.map(section_flow, (features, nexts))
    backward = lax.map(section_flow, (features, priors))
    valid_f = valid.astype(jnp.float32)
    link_all = valid_f * jnp.concatenate([valid_f[1:], jnp.zeros((1, TILES), jnp.float32)], axis=0)
    link_under = jnp.concatenate([jnp.zeros((1, TILES), jnp.float32), link_all[:-1]], axis=0)
    link_here = jnp.repeat(link_all, TILE_ROWS, axis=1)[:, None, :, None]
    link_below = jnp.repeat(link_under, TILE_ROWS, axis=1)[:, None, :, None]
    excess = link_here * forward - link_below * backward
    before = jnp.concatenate([jnp.zeros_like(excess[:1]), jnp.cumsum(excess[:-1], axis=0)], axis=0)
    displace = 0.5 * (before - link_below * backward)
    levels = jnp.arange(CLASSES, dtype=jnp.int32)
    stiff_field = lax.optimization_barrier(jnp.sum(jnp.where(class_map[None] == levels[:, None, None, None], stiffness[:, None, None, None], 0.0), axis=0))
    stiff_pad = jnp.pad(stiff_field, ((0, 0), (1, 1), (1, 1)))[:, None]
    for step_number in range(STEPS):
        disp_pad = jnp.pad(displace, ((0, 0), (0, 0), (1, 1), (1, 1)))
        elastic = elastic_term(disp_pad, stiff_pad)
        upper_disp = jnp.concatenate([displace[1:], jnp.zeros_like(displace[:1])], axis=0)
        lower_disp = jnp.concatenate([jnp.zeros_like(displace[:1]), displace[:-1]], axis=0)
        pull_up = link_here * spring(upper_disp - displace - forward)
        pull_down = link_below * spring(lower_disp - displace - backward)
        from_below = jnp.concatenate([jnp.zeros_like(pull_up[:1]), pull_up[:-1]], axis=0)
        from_above = jnp.concatenate([pull_down[1:], jnp.zeros_like(pull_down[:1])], axis=0)
        gradient = elastic - pull_up - pull_down + from_below + from_above
        displace = displace - step_size * gradient
    return (displace, forward)
```

```python
import functools

import jax
import jax.numpy as jnp
from jax import lax
from jax.experimental import pallas as pl
from jax.experimental.pallas import tpu as pltpu
from jax.sharding import PartitionSpec as P

RADIUS = 6
STEPS = 3


score_scale = 0.25
step_size = 0.1
saturation = 2.0


def padded_2(cells, sides, width):
    for axis, dim in sides:
        count = lax.axis_size(axis)
        ends = count - 1
        head = lax.slice_in_dim(cells, 0, width, axis=dim)
        tail = lax.slice_in_dim(cells, cells.shape[dim] - width, cells.shape[dim], axis=dim)
        cells = jnp.concatenate(
            [
                lax.ppermute(tail, axis, [(i, (i + 1) % count) for i in range(ends)]),
                cells,
                lax.ppermute(head, axis, [((i + 1) % count, i) for i in range(ends)]),
            ],
            axis=dim,
        )
    return cells


def passed_along(value, axis, steps):
    count = lax.axis_size(axis)
    initial, last = (max(0, -steps), min(count, count - steps))
    return lax.ppermute(value, axis, [(source, source + steps) for source in range(initial, last)])


def entering(shard, axis, combine, identity):
    length, here = (lax.axis_size(axis), lax.axis_index(axis))
    everything = lax.all_gather(shard, axis)
    start = jnp.broadcast_to(jnp.asarray(identity, shard.dtype), shard.shape)

    def step(k, before):
        reached = k < here
        new = combine(before, everything[k])
        return jnp.where(reached, new, before)

    return lax.fori_loop(0, length, step, start)


def shortened(shard):
    return jax.tree.map(lambda a: a.astype(jnp.bfloat16) if a.dtype == jnp.float32 else a, shard)


BLOCK = 4
SPAN = BLOCK + 2 * RADIUS
GROUP = 32
LOG2E = 1.4426950408889634
MASKED = -1e30


def flow_kernel(pairs, e_ref, l_ref, f_ref, b_ref, t_ref, bias_ref, o_ref):
    rows = f_ref.shape[1]
    channels, breadth = e_ref.shape[1], e_ref.shape[2]
    groups = rows // GROUP
    steps = breadth // BLOCK // (2 // groups)
    wide = t_ref.shape[3]
    lane = lax.broadcasted_iota(jnp.int32, (8, 128), 1)
    sub = lax.broadcasted_iota(jnp.int32, (8, 128), 0)
    qc = lane // GROUP
    qr = lane % BLOCK
    col_ok = []
    for half in range(2):
        kc = sub + 8 * half
        col_ok.append((kc >= qc) & (kc <= qc + 2 * RADIUS))
    edge = [k for k in range(SPAN) if k < BLOCK - 1 or k > 2 * RADIUS]
    for n, kr in enumerate(edge):
        row_ok = (qr <= kr) & (kr <= qr + 2 * RADIUS)
        for half in range(2):
            bias_ref[2 * n + half] = jnp.where(row_ok & col_ok[half], 0.0, MASKED)
    place = jnp.where(
        lax.broadcasted_iota(jnp.int32, (wide, breadth), 0)
        == lax.broadcasted_iota(jnp.int32, (wide, breadth), 1) + RADIUS,
        1.0,
        0.0,
    ).astype(jnp.bfloat16)
    per = GROUP // BLOCK
    for side, ref in enumerate((e_ref, l_ref)):
        for g in range(groups):
            for kr in range(0, SPAN, 2):
                pieces = [
                    ref[GROUP * g + kr + k + BLOCK * b] for k in range(2) for b in range(per)
                ]
                flat = jnp.concatenate(pieces, axis=0)
                out = lax.dot_general(
                    place, flat, (((1,), (1,)), ((), ())), preferred_element_type=jnp.float32
                )
                t_ref[side, g, kr] = out[:, :128]
                t_ref[side, g, kr + 1] = out[:, 128:]

    own = lax.broadcasted_iota(jnp.int32, (16, 128), 0) // BLOCK
    of = lax.broadcasted_iota(jnp.int32, (16, 128), 1) // channels
    zero_b = jnp.zeros((16, 128), jnp.bfloat16)
    sub_qr = sub % BLOCK
    for side in range(2):

        def step(i, carry):
            tiles = []
            for k in range(2):
                g = k if groups == 2 else 0
                base = i * BLOCK + (0 if groups == 2 else k * (breadth // 2))
                tiles.append((g, base))
            keys = []
            for kr in range(SPAN):
                keys.append(
                    jnp.concatenate(
                        [t_ref[1 - side, g, kr, pl.ds(base, SPAN), :] for g, base in tiles], axis=1
                    ).astype(jnp.bfloat16)
                )
            keys = jnp.concatenate(keys, axis=0)
            parts = []
            for k, (g, base) in enumerate(tiles):
                for c in range(BLOCK):
                    v = None
                    for r in range(BLOCK):
                        row = jnp.broadcast_to(
                            t_ref[side, g, RADIUS + r, pl.ds(base + RADIUS + c, 1), :], (8, 128)
                        )
                        v = row if v is None else jnp.where(sub_qr == r, row, v)
                    vb = jnp.concatenate([v, v], axis=0).astype(jnp.bfloat16)
                    for q in range(per // 4):
                        sel = jnp.where(of == own + 4 * q, vb, zero_b)
                        parts.append(
                            jnp.concatenate([sel, zero_b] if k == 0 else [zero_b, sel], axis=1)
                        )
            queries = jnp.concatenate(parts, axis=0)
            scores = lax.dot_general(
                keys, queries, (((1,), (1,)), ((), ())), preferred_element_type=jnp.float32
            )
            for k, (g, base) in enumerate(tiles):
                s = {}
                for kr in range(SPAN):
                    for half in range(2):
                        s[kr, half] = scores[
                            SPAN * kr + 8 * half : SPAN * kr + 8 * half + 8, 128 * k : 128 * k + 128
                        ]
                for n, kr in enumerate(edge):
                    for half in range(2):
                        s[kr, half] = s[kr, half] + bias_ref[2 * n + half]
                peak = []
                for half in range(2):
                    inner = functools.reduce(
                        jnp.maximum, [s[kr, half] for kr in range(SPAN) if kr not in edge]
                    )
                    inner = jnp.where(col_ok[half], inner, MASKED)
                    peak.append(
                        functools.reduce(jnp.maximum, [s[kr, half] for kr in edge] + [inner])
                    )
                top = jnp.max(jnp.maximum(peak[0], peak[1]), axis=0, keepdims=True)
                top = jnp.broadcast_to(top, (8, 128))
                total, slope = [], []
                for half in range(2):
                    acc = None
                    mom = None
                    for kr in reversed(range(SPAN)):
                        w = jnp.exp2((s[kr, half] - top) * (LOG2E * score_scale))
                        acc = w if acc is None else acc + w
                        if kr > 0:
                            mom = acc if mom is None else mom + acc
                    total.append(jnp.where(col_ok[half], acc, 0.0))
                    slope.append(jnp.where(col_ok[half], mom, 0.0))
                both = total[0] + total[1]
                den = jnp.sum(both, axis=0, keepdims=True)
                row_sum = jnp.sum(slope[0] + slope[1], axis=0, keepdims=True)
                col_sum = jnp.sum(
                    both * sub.astype(jnp.float32) + 8.0 * total[1], axis=0, keepdims=True
                )
                fr = row_sum / den - (qr[0:1] + RADIUS).astype(jnp.float32)
                fc = col_sum / den - (qc[0:1] + RADIUS).astype(jnp.float32)
                both_f = jnp.concatenate([fr, fc], axis=0)
                for c in range(BLOCK):
                    r = both_f if c == 0 else pltpu.roll(both_f, 128 - GROUP * c, 1)
                    o_ref[side, 0, g, pl.ds(base + c, 1), :] = r[0:1]
                    o_ref[side, 1, g, pl.ds(base + c, 1), :] = r[1:2]
            return carry

        lax.fori_loop(0, steps, step, 0)
    for side, ref in enumerate((f_ref, b_ref)):
        for comp in range(2):
            for g in range(groups):
                ref[comp, GROUP * g : GROUP * g + GROUP, :] = jnp.transpose(
                    o_ref[side, comp, g], (1, 0)
                )[:GROUP]


def flows(early, late):
    rows = early.shape[0] - 2 * RADIUS
    channels, breadth = early.shape[1:]
    groups = rows // GROUP
    wide = breadth + 16
    out = jax.ShapeDtypeStruct((2, rows, breadth), jnp.float32)
    return pl.pallas_call(
        functools.partial(flow_kernel, None),
        out_shape=(out, out),
        in_specs=[pl.BlockSpec(memory_space=pltpu.VMEM)] * 2,
        out_specs=(pl.BlockSpec(memory_space=pltpu.VMEM),) * 2,
        scratch_shapes=[
            pltpu.VMEM((2, groups, SPAN, wide, 128), jnp.float32),
            pltpu.VMEM((12, 8, 128), jnp.float32),
            pltpu.VMEM((2, 2, groups, breadth, 128), jnp.float32),
        ],
        compiler_params=pltpu.CompilerParams(vmem_limit_bytes=40 * 2**20),
        name="flows",
    )(early, late)


def widen(values_in, margin):
    padding = [(0, 0)] * (values_in.ndim - 1) + [(margin, margin)]
    return jnp.pad(values_in, padding)


def elastic_term(disp_pad, stiff_pad):
    middle = disp_pad[..., 1:-1, 1:-1]
    stiff_mid = stiff_pad[..., 1:-1, 1:-1]
    result = jnp.zeros_like(middle)
    for row_part, col_part in (
        (slice(2, None), slice(1, -1)),
        (slice(0, -2), slice(1, -1)),
        (slice(1, -1), slice(2, None)),
        (slice(1, -1), slice(0, -2)),
    ):
        neighbour_stiff = stiff_pad[..., row_part, col_part]
        result = result + 0.5 * (stiff_mid + neighbour_stiff) * (
            middle - disp_pad[..., row_part, col_part]
        )
    return result


def spring(vector):
    return vector / jnp.sqrt(
        1.0 + jnp.sum(vector * vector, axis=-3, keepdims=True) / (saturation * saturation)
    )


def add_pair(earlier, later):
    return earlier + later


def on_device(features, class_map, stiffness, valid):
    center = jnp.transpose(features[0], (1, 0, 2))
    section = lax.axis_index("gz")
    tile_index = lax.axis_index(("xy", "col"))
    column = lax.dynamic_slice_in_dim(valid, tile_index, 1, 1)[:, 0].astype(jnp.float32)
    link_all = column * jnp.concatenate([column[1:], jnp.zeros((1,), jnp.float32)])
    link_here = lax.dynamic_index_in_dim(link_all, section, 0, keepdims=False)
    link_below = jnp.where(
        section > 0,
        lax.dynamic_index_in_dim(link_all, jnp.maximum(section - 1, 0), 0, keepdims=False),
        0.0,
    )
    padded = padded_2(center, ((("xy", "col"), 0),), RADIUS)
    upper_pad = passed_along(padded, "gz", -1)
    forward, ahead_flow = flows(padded, upper_pad)
    passed = passed_along(jnp.stack([forward, ahead_flow]), "gz", 1)
    prior_flow = passed[0]
    backward = passed[1]
    excess = link_here * forward - link_below * backward
    before = entering(excess, "gz", add_pair, jnp.zeros_like(excess))
    displace = 0.5 * (before - link_below * backward)
    levels = jnp.arange(stiffness.shape[0], dtype=jnp.int32)
    stiff_field = jnp.sum(
        jnp.where(class_map[0][None] == levels[:, None, None], stiffness[:, None, None], 0.0),
        axis=0,
    )
    stiff_pad = widen(padded_2(stiff_field, ((("xy", "col"), 0),), 1), 1)
    for step_number in range(STEPS):
        disp_pad = widen(padded_2(displace, ((("xy", "col"), 1),), 1), 1)
        elastic = elastic_term(disp_pad, stiff_pad)
        upper_disp = passed_along(shortened(displace), "gz", -1).astype(displace.dtype)
        lower_disp = passed_along(shortened(displace), "gz", 1).astype(displace.dtype)
        pull_up = link_here * spring(upper_disp - displace - forward)
        pull_down = link_below * spring(lower_disp - displace - backward)
        from_below = link_below * spring(displace - lower_disp - prior_flow)
        from_above = link_here * spring(displace - upper_disp - ahead_flow)
        gradient = elastic - pull_up - pull_down + from_below + from_above
        displace = displace - step_size * gradient
    return (displace[None], forward[None])


def solution(mesh):
    placed = (
        P(("groups", "gz"), None, ("xy", "col"), None),
        P(("groups", "gz"), ("xy", "col"), None),
        P(),
        P("groups", None),
    )
    return jax.shard_map(
        on_device,
        mesh=mesh,
        in_specs=placed,
        out_specs=(
            P(("groups", "gz"), None, ("xy", "col"), None),
            P(("groups", "gz"), None, ("xy", "col"), None),
        ),
        check_vma=False,
    )
```

```python
import functools

import jax
import jax.numpy as jnp
from jax import lax
from jax.experimental import pallas as pl
from jax.experimental.pallas import tpu as pltpu
from jax.sharding import PartitionSpec as P

RADIUS = 6
STEPS = 3
score_scale = 0.25
step_size = 0.1
saturation = 2.0
tile_axes = ("xy", "col")


def shifted(value, axis, steps):
    count = lax.axis_size(axis)
    initial, last = (max(0, -steps), min(count, count - steps))
    return lax.ppermute(value, axis, [(source, source + steps) for source in range(initial, last)])


BLOCK = 4
SPAN = BLOCK + 2 * RADIUS
GROUP = 32
LOG2E = 1.4426950408889634
MASKED = -1e30


def flow_kernel(e_ref, l_ref, f_ref, b_ref, t_ref, bias_ref, o_ref, s0_ref, s1_ref, s2_ref, s3_ref, w_ref):

    rows = f_ref.shape[1]
    channels, breadth = e_ref.shape[1], e_ref.shape[2]
    groups = rows // GROUP
    steps = breadth // BLOCK // (2 // groups)
    wide = t_ref.shape[3]
    lane = lax.broadcasted_iota(jnp.int32, (8, 128), 1)
    sub = lax.broadcasted_iota(jnp.int32, (8, 128), 0)
    qc = lane // GROUP
    qr = lane % GROUP // (GROUP // BLOCK)
    col_ok = []
    for half in range(2):
        kc = sub + 8 * half
        col_ok.append((kc >= qc) & (kc <= qc + 2 * RADIUS))
    edge = [k for k in range(SPAN) if k < BLOCK - 1 or k > 2 * RADIUS]
    for n, kr in enumerate(edge):
        row_ok = (qr <= kr) & (kr <= qr + 2 * RADIUS)
        for half in range(2):
            bias_ref[2 * n + half] = jnp.where(row_ok & col_ok[half], 0.0, MASKED)
    place = jnp.where(
        lax.broadcasted_iota(jnp.int32, (wide, breadth), 0)
        == lax.broadcasted_iota(jnp.int32, (wide, breadth), 1) + RADIUS,
        1.0,
        0.0,
    ).astype(jnp.bfloat16)
    per = GROUP // BLOCK
    for side, ref in enumerate((e_ref, l_ref)):
        for g in range(groups):
            for kr in range(0, SPAN, 2):
                pieces = [
                    ref[GROUP * g + kr + k + BLOCK * b] for k in range(2) for b in range(per)
                ]
                flat = jnp.concatenate(pieces, axis=0)
                out = lax.dot_general(
                    place, flat, (((1,), (1,)), ((), ())), preferred_element_type=jnp.float32
                )
                t_ref[side, g, kr] = out[:, :128]
                t_ref[side, g, kr + 1] = out[:, 128:]

    diagonal = lane // channels == sub
    zero_b = jnp.zeros((16, 128), jnp.bfloat16)
    for side in range(2):

        def tiles_of(i):
            tiles = []
            for k in range(2):
                g = k if groups == 2 else 0
                base = i * BLOCK + (0 if groups == 2 else k * (breadth // 2))
                tiles.append((g, base))
            return tiles

        def score(i, s_ref):
            tiles = tiles_of(i)
            keys = []
            for kr in range(SPAN):
                keys.append(
                    jnp.concatenate(
                        [t_ref[1 - side, g, kr, pl.ds(base, SPAN), :] for g, base in tiles], axis=1
                    ).astype(jnp.bfloat16)
                )
            keys = jnp.concatenate(keys, axis=0)
            parts = []
            for k, (g, base) in enumerate(tiles):
                for c in range(BLOCK):
                    for r in range(0, BLOCK, 2):
                        pair = [
                            jnp.where(
                                diagonal,
                                t_ref[side, g, RADIUS + r + m, pl.ds(base + RADIUS + c, 1), :],
                                0.0,
                            )
                            for m in range(2)
                        ]
                        sel = jnp.concatenate(pair, axis=0).astype(jnp.bfloat16)
                        parts.append(
                            jnp.concatenate([sel, zero_b] if k == 0 else [zero_b, sel], axis=1)
                        )
            queries = jnp.concatenate(parts, axis=0)
            s_ref[...] = lax.dot_general(
                keys, queries, (((1,), (1,)), ((), ())), preferred_element_type=jnp.float32
            )

        def settle(i, s_ref):
            for k, (g, base) in enumerate(tiles_of(i)):
                s = {}
                for kr in range(SPAN):
                    for half in range(2):
                        s[kr, half] = s_ref[
                            SPAN * kr + 8 * half : SPAN * kr + 8 * half + 8, 128 * k : 128 * k + 128
                        ]
                for n, kr in enumerate(edge):
                    for half in range(2):
                        s[kr, half] = s[kr, half] + bias_ref[2 * n + half]
                peak = []
                for half in range(2):
                    inner = functools.reduce(
                        jnp.maximum, [s[kr, half] for kr in range(SPAN) if kr not in edge]
                    )
                    inner = jnp.where(col_ok[half], inner, MASKED)
                    peak.append(
                        functools.reduce(jnp.maximum, [s[kr, half] for kr in edge] + [inner])
                    )
                top = jnp.max(jnp.maximum(peak[0], peak[1]), axis=0, keepdims=True)
                top = jnp.broadcast_to(top, (8, 128))
                total, slope = [], []
                for half in range(2):
                    acc = None
                    mom = None
                    for kr in reversed(range(SPAN)):
                        w = jnp.exp2((s[kr, half] - top) * (LOG2E * score_scale))
                        acc = w if acc is None else acc + w
                        if kr > 0:
                            mom = acc if mom is None else mom + acc
                    total.append(jnp.where(col_ok[half], acc, 0.0))
                    slope.append(jnp.where(col_ok[half], mom, 0.0))
                both = total[0] + total[1]
                den = jnp.sum(both, axis=0, keepdims=True)
                row_sum = jnp.sum(slope[0] + slope[1], axis=0, keepdims=True)
                col_sum = jnp.sum(
                    both * sub.astype(jnp.float32) + 8.0 * total[1], axis=0, keepdims=True
                )
                fr = row_sum / den - (qr[0:1] + RADIUS).astype(jnp.float32)
                fc = col_sum / den - (qc[0:1] + RADIUS).astype(jnp.float32)
                both_f = jnp.concatenate([fr, fc], axis=0)
                for c in range(BLOCK):
                    r = both_f if c == 0 else pltpu.roll(both_f, 128 - GROUP * c, 1)
                    o_ref[side, 0, g, pl.ds(base + c, 1), :] = r[0:1]
                    o_ref[side, 1, g, pl.ds(base + c, 1), :] = r[1:2]

        def step(j, carry):
            last = steps - 1
            score(4 * j + 2, s2_ref)
            settle(4 * j, s0_ref)
            score(4 * j + 3, s3_ref)
            settle(4 * j + 1, s1_ref)
            score(jnp.minimum(4 * j + 4, last), s0_ref)
            settle(4 * j + 2, s2_ref)
            score(jnp.minimum(4 * j + 5, last), s1_ref)
            settle(4 * j + 3, s3_ref)
            return carry

        score(0, s0_ref)
        score(1, s1_ref)
        lax.fori_loop(0, steps // 4, step, 0)
    for side, ref in enumerate((f_ref, b_ref)):
        for comp in range(2):
            for g in range(groups):
                turned = jnp.transpose(o_ref[side, comp, g], (1, 0))
                for t in range(breadth // 128):
                    for r in range(BLOCK):
                        w_ref[side, comp, g, t, pl.ds(r, per, stride=BLOCK), :] = turned[
                            per * r : per * r + per, 128 * t : 128 * t + 128
                        ]
                    ref[comp, GROUP * g : GROUP * g + GROUP, 128 * t : 128 * t + 128] = w_ref[
                        side, comp, g, t
                    ]


def flows(early, late):
    rows = early.shape[0] - 2 * RADIUS
    channels, breadth = early.shape[1:]
    groups = rows // GROUP
    wide = breadth + 16
    out = jax.ShapeDtypeStruct((2, rows, breadth), jnp.float32)
    return pl.pallas_call(
        flow_kernel,
        out_shape=(out, out),
        in_specs=[pl.BlockSpec(memory_space=pltpu.VMEM)] * 2,
        out_specs=(pl.BlockSpec(memory_space=pltpu.VMEM),) * 2,
        scratch_shapes=[
            pltpu.VMEM((2, groups, SPAN, wide, 128), jnp.float32),
            pltpu.VMEM((12, 8, 128), jnp.float32),
            pltpu.VMEM((2, 2, groups, breadth, 128), jnp.float32),
            pltpu.VMEM((SPAN * SPAN, 256), jnp.float32),
            pltpu.VMEM((SPAN * SPAN, 256), jnp.float32),
            pltpu.VMEM((SPAN * SPAN, 256), jnp.float32),
            pltpu.VMEM((SPAN * SPAN, 256), jnp.float32),
            pltpu.VMEM((2, 2, groups, breadth // 128, GROUP, 128), jnp.float32),
        ],
        compiler_params=pltpu.CompilerParams(vmem_limit_bytes=40 * 2**20),
        name="flows",
    )(early, late)


def spring(vector):
    squares = jnp.sum(vector * vector, axis=0, keepdims=True)
    return vector / jnp.sqrt(1.0 + squares / (saturation * saturation))


def relaxed(u, stiff, inside):
    rows = u.shape[1]
    sides = ((0, 0), (0, 0), (1, 1))
    u_wide = jnp.pad(u, sides)
    s_wide = jnp.pad(stiff[None], sides)
    u_mid, s_mid = u[:, 1:-1], stiff[None, 1:-1]
    total = jnp.zeros_like(u_mid)
    for r, c in ((2, 1), (0, 1), (1, 2), (1, 0)):
        row_part, col_part = slice(r, r + rows - 2), slice(c, c + u.shape[2])
        total = total + 0.5 * (s_mid + s_wide[:, row_part, col_part]) * (
            u_mid - u_wide[:, row_part, col_part]
        )
    return jnp.where(inside[None, 1:-1], u_mid - step_size * total, 0.0)


def trim(rows, value):
    return value[..., rows : value.shape[-2] - rows, :]


def force(up, down, here, below, forward, ahead, prior, backward):
    pulls = here * (spring(up - forward) - spring(-up - ahead))
    return step_size * (pulls + below * (spring(down - backward) - spring(-down - prior)))


def prefix(pair_sum):
    count = lax.axis_size("gz")
    reach = 2
    while reach < count - 2:
        pair_sum = pair_sum + shifted(pair_sum, "gz", reach)
        reach *= 2
    return shifted(pair_sum, "gz", 2)


def on_device(features, class_map, stiffness, valid):
    center = jnp.transpose(features[0], (1, 0, 2))
    height, channels, breadth = center.shape
    codes = (class_map[0] + 1).astype(jnp.bfloat16).reshape(-1, channels, breadth)
    section = lax.axis_index("gz")
    tile = lax.axis_index(tile_axes)

    top = jnp.concatenate([center[:RADIUS], codes[:1]])
    bottom = jnp.concatenate([center[-RADIUS:], codes[-1:]])
    before = shifted(bottom, tile_axes, 1)
    after = shifted(top, tile_axes, -1)
    padded = jnp.concatenate([before[:RADIUS], center, after[:RADIUS]])
    own_codes = jnp.concatenate(
        [
            before[RADIUS, -STEPS:],
            codes.reshape(height, breadth),
            after[RADIUS, :STEPS],
        ]
    )
    spare = -own_codes.shape[0] % channels
    packed = jnp.pad(own_codes, ((0, spare), (0, 0))).reshape(-1, channels, breadth)
    upper = shifted(jnp.concatenate([padded, packed]), "gz", -1)
    upper_pad = upper[: padded.shape[0]]
    upper_codes = upper[padded.shape[0] :].reshape(-1, breadth)[: own_codes.shape[0]]
    forward, ahead = flows(padded, upper_pad)

    both = jnp.concatenate([forward, ahead])
    both = jnp.concatenate(
        [
            shifted(both[:, -STEPS:], tile_axes, 1),
            both,
            shifted(both[:, :STEPS], tile_axes, -1),
        ],
        axis=1,
    )
    message = jnp.concatenate([both, own_codes[None].astype(jnp.float32)])
    lower = shifted(message, "gz", 1)
    fwd, ahd = both[:2], both[2:]
    pri, bwd = lower[:2], lower[2:4]

    def stiff_of(code):
        levels = jnp.arange(stiffness.shape[0], dtype=jnp.float32)[:, None, None] + 1.0
        code = code.astype(jnp.float32)
        field = jnp.sum(jnp.where(code[None] == levels, stiffness[:, None, None], 0.0), axis=0)
        return field, code > 0.0

    stiff, inside = stiff_of(own_codes)
    stiff_up, inside_up = stiff_of(upper_codes)
    stiff_down, inside_down = stiff_of(lower[4])

    sound = jnp.pad(valid.astype(jnp.float32), ((1, 1), (1, 1)))
    near = lax.dynamic_slice(sound, (section, tile), (3, 3))
    links = near[:-1] * near[1:]
    by_row = jnp.repeat(
        links, jnp.array([STEPS, height, STEPS]), axis=1, total_repeat_length=height + 2 * STEPS
    )
    below, here = by_row[0][None, :, None], by_row[1][None, :, None]

    gain = here * (fwd - ahd)
    gain_below = below * (pri - bwd)
    start = 0.5 * (prefix(gain + gain_below) + gain_below)
    pull = force(0.5 * gain, -0.5 * gain_below, here, below, fwd, ahd, pri, bwd)
    sent = trim(2, pull).astype(jnp.bfloat16)
    pull_up = shifted(sent, "gz", -1).astype(jnp.float32)
    pull_down = shifted(sent, "gz", 1).astype(jnp.float32)

    start_up = start + 0.5 * gain
    start_down = start - 0.5 * gain_below
    first = relaxed(start, stiff, inside) + trim(1, pull)
    first_up = relaxed(trim(1, start_up), trim(1, stiff_up), trim(1, inside_up)) + pull_up
    first_down = (
        relaxed(trim(1, start_down), trim(1, stiff_down), trim(1, inside_down)) + pull_down
    )
    mid = trim(1, first)
    fields = [trim(2, x) for x in (here, below, fwd, ahd, pri, bwd)]
    second = relaxed(first, trim(1, stiff), trim(1, inside)) + force(
        first_up - mid, first_down - mid, *fields
    )
    change = trim(1, second) - trim(3, start)
    change = change.astype(jnp.bfloat16)
    last_up = trim(3, start_up) + shifted(change, "gz", -1).astype(jnp.float32)
    last_down = trim(3, start_down) + shifted(change, "gz", 1).astype(jnp.float32)
    fields = [trim(1, x) for x in fields]
    mid = trim(1, second)
    third = relaxed(second, trim(2, stiff), trim(2, inside)) + force(
        last_up - mid, last_down - mid, *fields
    )
    return (third[None], forward[None])


def solution(mesh):
    placed = (
        P(("groups", "gz"), None, tile_axes, None),
        P(("groups", "gz"), tile_axes, None),
        P(),
        P("groups", None),
    )
    return jax.shard_map(
        on_device,
        mesh=mesh,
        in_specs=placed,
        out_specs=(P(("groups", "gz"), None, tile_axes, None),) * 2,
        check_vma=False,
    )
```

```python
import functools

import jax
import jax.numpy as jnp
from jax import lax
from jax.experimental import pallas as pl
from jax.experimental.pallas import tpu as pltpu
from jax.sharding import PartitionSpec as P

RADIUS = 6
STEPS = 3
score_scale = 0.25
step_size = 0.1
saturation = 2.0
tile_axes = ("xy", "col")


def ringed(value, axis, steps):
    count = lax.axis_size(axis)
    return lax.ppermute(value, axis, [(i, (i + steps) % count) for i in range(count)])


BLOCK = 4
SPAN = BLOCK + 2 * RADIUS
GROUP = 32
LOG2E = 1.4426950408889634
MASKED = -1e30


def flow_kernel(
    early_rows, late_rows, n_early, live_ref, *refs
):
    n_in = n_early + 1 + max(i for i, _ in late_rows)
    ins, out_ref = refs[:n_in], refs[n_in]
    t_ref, bias_ref, o_ref, s0_ref, s1_ref, s2_ref, s3_ref, w_ref = refs[n_in + 1 :]
    channels, breadth = ins[0].shape[1:]
    groups = 1
    steps = breadth // BLOCK // 2
    wide = t_ref.shape[3]
    lane = lax.broadcasted_iota(jnp.int32, (8, 128), 1)
    sub = lax.broadcasted_iota(jnp.int32, (8, 128), 0)
    qc = lane // GROUP
    qr = lane % GROUP // (GROUP // BLOCK)
    col_ok = []
    for half in range(2):
        kc = sub + 8 * half
        col_ok.append((kc >= qc) & (kc <= qc + 2 * RADIUS))
    edge = [k for k in range(SPAN) if k < BLOCK - 1 or k > 2 * RADIUS]
    for n, kr in enumerate(edge):
        row_ok = (qr <= kr) & (kr <= qr + 2 * RADIUS)
        for half in range(2):
            bias_ref[2 * n + half] = jnp.where(row_ok & col_ok[half], 0.0, MASKED)
    place = jnp.where(
        lax.broadcasted_iota(jnp.int32, (wide, breadth), 0)
        == lax.broadcasted_iota(jnp.int32, (wide, breadth), 1) + RADIUS,
        1.0,
        0.0,
    ).astype(jnp.bfloat16)
    per = GROUP // BLOCK
    for side, (offset, table) in enumerate(((0, early_rows), (n_early, late_rows))):
        for g in range(groups):
            for kr in range(0, SPAN, 2):
                pieces = []
                for k in range(2):
                    for b in range(per):
                        which, row = table[SPAN * b + kr + k]
                        pieces.append(ins[offset + which][row])
                flat = jnp.concatenate(pieces, axis=0)
                out = lax.dot_general(
                    place, flat, (((1,), (1,)), ((), ())), preferred_element_type=jnp.float32
                )
                t_ref[side, g, kr] = out[:, :128]
                t_ref[side, g, kr + 1] = out[:, 128:]

    diagonal = lane // channels == sub
    zero_b = jnp.zeros((16, 128), jnp.bfloat16)
    for side in range(2):

        def tiles_of(i):
            tiles = []
            for k in range(2):
                g = 0
                base = i * BLOCK + k * (breadth // 2)
                tiles.append((g, base))
            return tiles

        def score(i, s_ref):
            tiles = tiles_of(i)
            keys = []
            for kr in range(SPAN):
                keys.append(
                    jnp.concatenate(
                        [t_ref[1 - side, g, kr, pl.ds(base, SPAN), :] for g, base in tiles], axis=1
                    ).astype(jnp.bfloat16)
                )
            keys = jnp.concatenate(keys, axis=0)
            parts = []
            for k, (g, base) in enumerate(tiles):
                for c in range(BLOCK):
                    for r in range(0, BLOCK, 2):
                        pair = [
                            jnp.where(
                                diagonal,
                                t_ref[side, g, RADIUS + r + m, pl.ds(base + RADIUS + c, 1), :],
                                0.0,
                            )
                            for m in range(2)
                        ]
                        sel = jnp.concatenate(pair, axis=0).astype(jnp.bfloat16)
                        parts.append(
                            jnp.concatenate([sel, zero_b] if k == 0 else [zero_b, sel], axis=1)
                        )
            queries = jnp.concatenate(parts, axis=0)
            s_ref[...] = lax.dot_general(
                keys, queries, (((1,), (1,)), ((), ())), preferred_element_type=jnp.float32
            )

        def settle(i, s_ref):
            for k, (g, base) in enumerate(tiles_of(i)):
                s = {}
                for kr in range(SPAN):
                    for half in range(2):
                        s[kr, half] = s_ref[
                            SPAN * kr + 8 * half : SPAN * kr + 8 * half + 8, 128 * k : 128 * k + 128
                        ]
                for n, kr in enumerate(edge):
                    for half in range(2):
                        s[kr, half] = s[kr, half] + bias_ref[2 * n + half]
                peak = []
                for half in range(2):
                    inner = functools.reduce(
                        jnp.maximum, [s[kr, half] for kr in range(SPAN) if kr not in edge]
                    )
                    inner = jnp.where(col_ok[half], inner, MASKED)
                    peak.append(
                        functools.reduce(jnp.maximum, [s[kr, half] for kr in edge] + [inner])
                    )
                top = jnp.max(jnp.maximum(peak[0], peak[1]), axis=0, keepdims=True)
                top = jnp.broadcast_to(top, (8, 128))
                total, slope = [], []
                for half in range(2):
                    acc = None
                    mom = None
                    for kr in reversed(range(SPAN)):
                        w = jnp.exp2((s[kr, half] - top) * (LOG2E * score_scale))
                        acc = w if acc is None else acc + w
                        if kr > 0:
                            mom = acc if mom is None else mom + acc
                    total.append(jnp.where(col_ok[half], acc, 0.0))
                    slope.append(jnp.where(col_ok[half], mom, 0.0))
                both = total[0] + total[1]
                den = jnp.sum(both, axis=0, keepdims=True)
                row_sum = jnp.sum(slope[0] + slope[1], axis=0, keepdims=True)
                col_sum = jnp.sum(
                    both * sub.astype(jnp.float32) + 8.0 * total[1], axis=0, keepdims=True
                )
                fr = row_sum / den - (qr[0:1] + RADIUS).astype(jnp.float32)
                fc = col_sum / den - (qc[0:1] + RADIUS).astype(jnp.float32)
                both_f = jnp.concatenate([fr, fc], axis=0)
                for c in range(BLOCK):
                    r = both_f if c == 0 else pltpu.roll(both_f, 128 - GROUP * c, 1)
                    o_ref[side, 0, g, pl.ds(base + c, 1), :] = r[0:1]
                    o_ref[side, 1, g, pl.ds(base + c, 1), :] = r[1:2]

        def step(j, carry):
            last = steps - 1
            score(4 * j + 2, s2_ref)
            settle(4 * j, s0_ref)
            score(4 * j + 3, s3_ref)
            settle(4 * j + 1, s1_ref)
            score(jnp.minimum(4 * j + 4, last), s0_ref)
            settle(4 * j + 2, s2_ref)
            score(jnp.minimum(4 * j + 5, last), s1_ref)
            settle(4 * j + 3, s3_ref)
            return carry

        score(0, s0_ref)
        score(1, s1_ref)
        lax.fori_loop(0, steps // 4, step, 0)
    live = live_ref[0]
    for side in range(2):
        for comp in range(2):
            turned = jnp.transpose(o_ref[side, comp, 0], (1, 0)) * live
            for t in range(breadth // 128):
                for r in range(BLOCK):
                    w_ref[side, comp, t, pl.ds(r, per, stride=BLOCK), :] = turned[
                        per * r : per * r + per, 128 * t : 128 * t + 128
                    ]
                out_ref[2 * side + comp, :, 128 * t : 128 * t + 128] = w_ref[side, comp, t]


def flows(live, early, late, early_at, late_at, starts):
    channels, breadth = early[0].shape[1:]
    wide = breadth + 16
    tables = [
        [at(start - RADIUS + k) for start in starts for k in range(SPAN)]
        for at in (early_at, late_at)
    ]
    cells = GROUP * breadth
    return pl.pallas_call(
        functools.partial(flow_kernel, *tables, len(early)),
        out_shape=jax.ShapeDtypeStruct((4, GROUP, breadth), jnp.float32),
        in_specs=[pl.BlockSpec(memory_space=pltpu.SMEM)]
        + [pl.BlockSpec(memory_space=pltpu.VMEM)] * (len(early) + len(late)),
        out_specs=pl.BlockSpec(memory_space=pltpu.VMEM),
        scratch_shapes=[
            pltpu.VMEM((2, 1, SPAN, wide, 128), jnp.float32),
            pltpu.VMEM((12, 8, 128), jnp.float32),
            pltpu.VMEM((2, 2, 1, breadth, 128), jnp.float32),
        ]
        + [pltpu.VMEM((SPAN * SPAN, 256), jnp.float32)] * 4
        + [pltpu.VMEM((2, 2, breadth // 128, GROUP, 128), jnp.float32)],
        compiler_params=pltpu.CompilerParams(vmem_limit_bytes=24 * 2**20),
        cost_estimate=pl.CostEstimate(
            flops=2 * cells * SPAN * SPAN * 2 * 256, bytes_accessed=2**22, transcendentals=2 * cells * SPAN * SPAN
        ),
        name="flows",
    )(live, *early, *late)


def spring(vector):
    squares = jnp.sum(vector * vector, axis=0, keepdims=True)
    return vector / jnp.sqrt(1.0 + squares / (saturation * saturation))


def relaxed(u, stiff, inside):
    rows = u.shape[1]
    sides = ((0, 0), (0, 0), (1, 1))
    u_wide = jnp.pad(u, sides)
    s_wide = jnp.pad(stiff[None], sides)
    u_mid, s_mid = u[:, 1:-1], stiff[None, 1:-1]
    total = jnp.zeros_like(u_mid)
    for r, c in ((2, 1), (0, 1), (1, 2), (1, 0)):
        row_part, col_part = slice(r, r + rows - 2), slice(c, c + u.shape[2])
        total = total + 0.5 * (s_mid + s_wide[:, row_part, col_part]) * (
            u_mid - u_wide[:, row_part, col_part]
        )
    return jnp.where(inside[None, 1:-1], u_mid - step_size * total, 0.0)


def trim(rows, value):
    return value[..., rows : value.shape[-2] - rows, :]


def force(up, down, here, below, forward, ahead, prior, backward):
    pulls = here * (spring(up - forward) - spring(-up - ahead))
    return step_size * (pulls + below * (spring(down - backward) - spring(-down - prior)))


def prefix(pair_sum, section):
    count = lax.axis_size("gz")

    def earlier(value, steps):
        return jnp.where(section >= steps, ringed(value, "gz", steps), 0.0)

    reach = 2
    while reach < count - 2:
        pair_sum = pair_sum + earlier(pair_sum, reach)
        reach *= 2
    return earlier(pair_sum, 2)


def on_device(features, class_map, stiffness, valid):
    center = jnp.transpose(features[0], (1, 0, 2))
    height, channels, breadth = center.shape
    section, sections = lax.axis_index("gz"), lax.axis_size("gz")
    tile, tiles = lax.axis_index(tile_axes), lax.axis_size(tile_axes)
    quarter = height // 4
    low, high = quarter - RADIUS, height - quarter + RADIUS

    upper_mid = ringed(center[low:high], "gz", -1)

    codes = (class_map[0] + 1).astype(jnp.bfloat16).reshape(-1, channels, breadth)
    top = jnp.concatenate([center[:RADIUS], codes[:1]])
    bottom = jnp.concatenate([center[-RADIUS:], codes[-1:]])
    nothing = jnp.zeros_like(top)
    before = jnp.where(tile > 0, ringed(bottom, tile_axes, 1), nothing)
    after = jnp.where(tile < tiles - 1, ringed(top, tile_axes, -1), nothing)
    own_codes = jnp.concatenate(
        [before[RADIUS, -STEPS:], codes.reshape(height, breadth), after[RADIUS, :STEPS]]
    )
    spare = -own_codes.shape[0] % channels
    packed = jnp.pad(own_codes, ((0, spare), (0, 0))).reshape(-1, channels, breadth)
    upper_out = ringed(
        jnp.concatenate([before[:RADIUS], center[:low], center[high:], after[:RADIUS], packed]),
        "gz",
        -1,
    )
    outer = low + RADIUS
    upper_codes = upper_out[2 * outer :].reshape(-1, breadth)[: own_codes.shape[0]]

    def own_at(row):
        if row < 0:
            return 1, row + RADIUS
        return (0, row) if row < height else (2, row - height)

    def upper_at(row):
        if low <= row < high:
            return 0, row - low
        return (1, row + RADIUS) if row < low else (1, row - high + outer)

    live = jnp.where(section < sections - 1, 1.0, 0.0)[None]
    middle_rows = range(quarter, height - quarter, BLOCK)
    middle = flows(live, [center], [upper_mid], own_at, upper_at, middle_rows)
    lower_mid = ringed(
        jnp.concatenate([middle.reshape(-1, breadth), own_codes.astype(jnp.float32)]), "gz", 1
    )
    outer_rows = [*range(0, quarter, BLOCK), *range(height - quarter, height, BLOCK)]
    outside = flows(
        live, [center, before, after], [upper_mid, upper_out], own_at, upper_at, outer_rows
    )

    head, tail = outside[:, :quarter], outside[:, quarter:]
    head = jnp.concatenate([ringed(tail[:, -STEPS:], tile_axes, 1), head], axis=1)
    tail = jnp.concatenate([tail, ringed(outside[:, :STEPS], tile_axes, -1)], axis=1)
    lower_out = ringed(jnp.concatenate([head, tail], axis=1), "gz", 1)
    both = jnp.concatenate([head, middle, tail], axis=1)
    n_mid = middle.shape[0] * middle.shape[1]
    lower = jnp.concatenate(
        [
            lower_out[:, : head.shape[1]],
            lower_mid[:n_mid].reshape(middle.shape),
            lower_out[:, head.shape[1] :],
        ],
        axis=1,
    )
    fwd, ahd = both[:2], both[2:]
    pri, bwd = lower[:2], lower[2:]
    forward = fwd[:, STEPS:-STEPS]

    def stiff_of(code):
        levels = jnp.arange(stiffness.shape[0], dtype=jnp.float32)[:, None, None] + 1.0
        code = code.astype(jnp.float32)
        field = jnp.sum(jnp.where(code[None] == levels, stiffness[:, None, None], 0.0), axis=0)
        return field, code > 0.0

    stiff, inside = stiff_of(own_codes)
    stiff_up, inside_up = stiff_of(upper_codes)
    stiff_down, inside_down = stiff_of(lower_mid[n_mid:])

    sound = jnp.pad(valid.astype(jnp.float32), ((1, 1), (1, 1)))
    near = lax.dynamic_slice(sound, (section, tile), (3, 3))
    links = near[:-1] * near[1:]
    by_row = jnp.concatenate(
        [
            jnp.broadcast_to(links[:, k : k + 1], (2, count))
            for k, count in enumerate((STEPS, height, STEPS))
        ],
        axis=1,
    )
    below, here = by_row[0][None, :, None], by_row[1][None, :, None]

    gain = here * (fwd - ahd)
    gain_below = below * (pri - bwd)
    start = 0.5 * (prefix(gain + gain_below, section) + gain_below)
    pull = force(0.5 * gain, -0.5 * gain_below, here, below, fwd, ahd, pri, bwd)
    sent = trim(2, pull).astype(jnp.bfloat16)
    pull_up = ringed(sent, "gz", -1).astype(jnp.float32)
    pull_down = ringed(sent, "gz", 1).astype(jnp.float32)

    start_up = start + 0.5 * gain
    start_down = start - 0.5 * gain_below
    first = relaxed(start, stiff, inside) + trim(1, pull)
    first_up = relaxed(trim(1, start_up), trim(1, stiff_up), trim(1, inside_up)) + pull_up
    first_down = (
        relaxed(trim(1, start_down), trim(1, stiff_down), trim(1, inside_down)) + pull_down
    )
    mid = trim(1, first)
    fields = [trim(2, x) for x in (here, below, fwd, ahd, pri, bwd)]
    second = relaxed(first, trim(1, stiff), trim(1, inside)) + force(
        first_up - mid, first_down - mid, *fields
    )
    change = trim(1, second) - trim(3, start)
    change = change.astype(jnp.bfloat16)
    last_up = trim(3, start_up) + ringed(change, "gz", -1).astype(jnp.float32)
    last_down = trim(3, start_down) + ringed(change, "gz", 1).astype(jnp.float32)
    fields = [trim(1, x) for x in fields]
    mid = trim(1, second)
    third = relaxed(second, trim(2, stiff), trim(2, inside)) + force(
        last_up - mid, last_down - mid, *fields
    )
    return (third[None], forward[None])


def solution(mesh):
    placed = (
        P(("groups", "gz"), None, tile_axes, None),
        P(("groups", "gz"), tile_axes, None),
        P(),
        P("groups", None),
    )
    return jax.shard_map(
        on_device,
        mesh=mesh,
        in_specs=placed,
        out_specs=(P(("groups", "gz"), None, tile_axes, None),) * 2,
        check_vma=False,
    )
```

```python
import functools

import jax
import jax.numpy as jnp
from jax import lax
from jax.experimental import pallas as pl
from jax.experimental.pallas import tpu as pltpu
from jax.sharding import PartitionSpec as P

RADIUS = 6
STEPS = 3
score_scale = 0.25
step_size = 0.1
saturation = 2.0
tile_axes = ("xy", "col")


def ringed(value, axis, steps):
    count = lax.axis_size(axis)
    return lax.ppermute(value, axis, [(i, (i + steps) % count) for i in range(count)])


BLOCK = 4
SPAN = BLOCK + 2 * RADIUS
GROUP = 32
LOG2E = 1.4426950408889634
MASKED = -1e30


def flow_kernel(
    early_rows, late_rows, n_early, live_ref, *refs
):
    n_in = n_early + 1 + max(i for i, _ in late_rows)
    ins, out_ref = refs[:n_in], refs[n_in]
    t_ref, bias_ref, o_ref, s0_ref, s1_ref, s2_ref, s3_ref, w_ref = refs[n_in + 1 :]
    channels, breadth = ins[0].shape[1:]
    groups = 1
    steps = breadth // BLOCK // 2
    wide = t_ref.shape[3]
    lane = lax.broadcasted_iota(jnp.int32, (8, 128), 1)
    sub = lax.broadcasted_iota(jnp.int32, (8, 128), 0)
    qc = lane // GROUP
    qr = lane % GROUP // (GROUP // BLOCK)
    col_ok = []
    for half in range(2):
        kc = sub + 8 * half
        col_ok.append((kc >= qc) & (kc <= qc + 2 * RADIUS))
    edge = [k for k in range(SPAN) if k < BLOCK - 1 or k > 2 * RADIUS]
    for n, kr in enumerate(edge):
        row_ok = (qr <= kr) & (kr <= qr + 2 * RADIUS)
        for half in range(2):
            bias_ref[2 * n + half] = jnp.where(row_ok & col_ok[half], 0.0, MASKED)
    place = jnp.where(
        lax.broadcasted_iota(jnp.int32, (wide, breadth), 0)
        == lax.broadcasted_iota(jnp.int32, (wide, breadth), 1) + RADIUS,
        1.0,
        0.0,
    ).astype(jnp.bfloat16)
    per = GROUP // BLOCK
    for side, (offset, table) in enumerate(((0, early_rows), (n_early, late_rows))):
        for g in range(groups):
            for kr in range(0, SPAN, 2):
                pieces = []
                for k in range(2):
                    for b in range(per):
                        which, row = table[SPAN * b + kr + k]
                        pieces.append(ins[offset + which][row])
                flat = jnp.concatenate(pieces, axis=0)
                out = lax.dot_general(
                    place, flat, (((1,), (1,)), ((), ())), preferred_element_type=jnp.float32
                )
                t_ref[side, g, kr] = out[:, :128]
                t_ref[side, g, kr + 1] = out[:, 128:]

    diagonal = lane // channels == sub
    zero_b = jnp.zeros((16, 128), jnp.bfloat16)
    for side in range(2):

        def tiles_of(i):
            tiles = []
            for k in range(2):
                g = 0
                base = i * BLOCK + k * (breadth // 2)
                tiles.append((g, base))
            return tiles

        def score(i, s_ref):
            tiles = tiles_of(i)
            keys = []
            for kr in range(SPAN):
                keys.append(
                    jnp.concatenate(
                        [t_ref[1 - side, g, kr, pl.ds(base, SPAN), :] for g, base in tiles], axis=1
                    ).astype(jnp.bfloat16)
                )
            keys = jnp.concatenate(keys, axis=0)
            parts = []
            for k, (g, base) in enumerate(tiles):
                for c in range(BLOCK):
                    for r in range(0, BLOCK, 2):
                        pair = [
                            jnp.where(
                                diagonal,
                                t_ref[side, g, RADIUS + r + m, pl.ds(base + RADIUS + c, 1), :],
                                0.0,
                            )
                            for m in range(2)
                        ]
                        sel = jnp.concatenate(pair, axis=0).astype(jnp.bfloat16)
                        parts.append(
                            jnp.concatenate([sel, zero_b] if k == 0 else [zero_b, sel], axis=1)
                        )
            queries = jnp.concatenate(parts, axis=0)
            s_ref[...] = lax.dot_general(
                keys, queries, (((1,), (1,)), ((), ())), preferred_element_type=jnp.float32
            )

        def settle(i, s_ref):
            for k, (g, base) in enumerate(tiles_of(i)):
                s = {}
                for kr in range(SPAN):
                    for half in range(2):
                        s[kr, half] = s_ref[
                            SPAN * kr + 8 * half : SPAN * kr + 8 * half + 8, 128 * k : 128 * k + 128
                        ]
                for n, kr in enumerate(edge):
                    for half in range(2):
                        s[kr, half] = s[kr, half] + bias_ref[2 * n + half]
                peak = []
                for half in range(2):
                    inner = functools.reduce(
                        jnp.maximum, [s[kr, half] for kr in range(SPAN) if kr not in edge]
                    )
                    inner = jnp.where(col_ok[half], inner, MASKED)
                    peak.append(
                        functools.reduce(jnp.maximum, [s[kr, half] for kr in edge] + [inner])
                    )
                top = jnp.max(jnp.maximum(peak[0], peak[1]), axis=0, keepdims=True)
                top = jnp.broadcast_to(top, (8, 128))
                total, slope = [], []
                for half in range(2):
                    acc = None
                    mom = None
                    for kr in reversed(range(SPAN)):
                        w = jnp.exp2((s[kr, half] - top) * (LOG2E * score_scale))
                        acc = w if acc is None else acc + w
                        if kr > 0:
                            mom = acc if mom is None else mom + acc
                    total.append(jnp.where(col_ok[half], acc, 0.0))
                    slope.append(jnp.where(col_ok[half], mom, 0.0))
                both = total[0] + total[1]
                den = jnp.sum(both, axis=0, keepdims=True)
                row_sum = jnp.sum(slope[0] + slope[1], axis=0, keepdims=True)
                col_sum = jnp.sum(
                    both * sub.astype(jnp.float32) + 8.0 * total[1], axis=0, keepdims=True
                )
                fr = row_sum / den - (qr[0:1] + RADIUS).astype(jnp.float32)
                fc = col_sum / den - (qc[0:1] + RADIUS).astype(jnp.float32)
                both_f = jnp.concatenate([fr, fc], axis=0)
                for c in range(BLOCK):
                    r = both_f if c == 0 else pltpu.roll(both_f, 128 - GROUP * c, 1)
                    o_ref[side, 0, g, pl.ds(base + c, 1), :] = r[0:1]
                    o_ref[side, 1, g, pl.ds(base + c, 1), :] = r[1:2]

        def step(j, carry):
            last = steps - 1
            score(4 * j + 2, s2_ref)
            settle(4 * j, s0_ref)
            score(4 * j + 3, s3_ref)
            settle(4 * j + 1, s1_ref)
            score(jnp.minimum(4 * j + 4, last), s0_ref)
            settle(4 * j + 2, s2_ref)
            score(jnp.minimum(4 * j + 5, last), s1_ref)
            settle(4 * j + 3, s3_ref)
            return carry

        score(0, s0_ref)
        score(1, s1_ref)
        lax.fori_loop(0, steps // 4, step, 0)
    live = live_ref[0]
    for side in range(2):
        for comp in range(2):
            turned = jnp.transpose(o_ref[side, comp, 0], (1, 0)) * live
            for t in range(breadth // 128):
                for r in range(BLOCK):
                    w_ref[side, comp, t, pl.ds(r, per, stride=BLOCK), :] = turned[
                        per * r : per * r + per, 128 * t : 128 * t + 128
                    ]
                out_ref[2 * side + comp, :, 128 * t : 128 * t + 128] = w_ref[side, comp, t]


def flows(live, early, late, early_at, late_at, starts):
    channels, breadth = early[0].shape[1:]
    wide = breadth + 16
    tables = [
        [at(start - RADIUS + k) for start in starts for k in range(SPAN)]
        for at in (early_at, late_at)
    ]
    cells = GROUP * breadth
    return pl.pallas_call(
        functools.partial(flow_kernel, *tables, len(early)),
        out_shape=jax.ShapeDtypeStruct((4, GROUP, breadth), jnp.float32),
        in_specs=[pl.BlockSpec(memory_space=pltpu.SMEM)]
        + [pl.BlockSpec(memory_space=pltpu.VMEM)] * (len(early) + len(late)),
        out_specs=pl.BlockSpec(memory_space=pltpu.VMEM),
        scratch_shapes=[
            pltpu.VMEM((2, 1, SPAN, wide, 128), jnp.float32),
            pltpu.VMEM((12, 8, 128), jnp.float32),
            pltpu.VMEM((2, 2, 1, breadth, 128), jnp.float32),
        ]
        + [pltpu.VMEM((SPAN * SPAN, 256), jnp.float32)] * 4
        + [pltpu.VMEM((2, 2, breadth // 128, GROUP, 128), jnp.float32)],
        compiler_params=pltpu.CompilerParams(vmem_limit_bytes=24 * 2**20),
        cost_estimate=pl.CostEstimate(
            flops=2 * cells * SPAN * SPAN * 2 * 256, bytes_accessed=2**22, transcendentals=2 * cells * SPAN * SPAN
        ),
        name="flows",
    )(live, *early, *late)


def spring(vector):
    squares = jnp.sum(vector * vector, axis=0, keepdims=True)
    return vector / jnp.sqrt(1.0 + squares / (saturation * saturation))


def relaxed(u, stiff, inside):
    rows = u.shape[1]
    sides = ((0, 0), (0, 0), (1, 1))
    u_wide = jnp.pad(u, sides)
    s_wide = jnp.pad(stiff[None], sides)
    u_mid, s_mid = u[:, 1:-1], stiff[None, 1:-1]
    total = jnp.zeros_like(u_mid)
    for r, c in ((2, 1), (0, 1), (1, 2), (1, 0)):
        row_part, col_part = slice(r, r + rows - 2), slice(c, c + u.shape[2])
        total = total + 0.5 * (s_mid + s_wide[:, row_part, col_part]) * (
            u_mid - u_wide[:, row_part, col_part]
        )
    return jnp.where(inside[None, 1:-1], u_mid - step_size * total, 0.0)


def trim(rows, value):
    return value[..., rows : value.shape[-2] - rows, :]


def pair_part(apart, here, forward, ahead):
    return step_size * here * (spring(apart - forward) - spring(-apart - ahead))


def split(value):
    high = lax.reduce_precision(value, 8, 7)
    return [high.astype(jnp.bfloat16), (value - high).astype(jnp.bfloat16)]


def joined(parts):
    return parts[:2].astype(jnp.float32) + parts[2:4].astype(jnp.float32)


def running(gain, section):
    count = lax.axis_size("gz")
    reach = 1
    while count > 4 and reach < count - 2:
        more = jnp.where(section >= reach, ringed(gain, "gz", reach), 0.0)
        gain, reach = gain + more, 2 * reach
    return gain


def messages(flow, here, section):
    forward, ahead = flow[:2], flow[2:]
    gain = here * (forward - ahead)
    part = pair_part(0.5 * gain, here, forward, ahead).astype(jnp.bfloat16)
    halves = split(gain)
    to_next = jnp.concatenate([*halves, forward.astype(jnp.bfloat16)])
    to_second = jnp.concatenate([*split(running(gain, section)), part])
    return to_next, to_second, jnp.concatenate([part, *halves])


def on_device(features, class_map, stiffness, valid):
    center = jnp.transpose(features[0], (1, 0, 2))
    height, channels, breadth = center.shape
    section, sections = lax.axis_index("gz"), lax.axis_size("gz")
    tile, tiles = lax.axis_index(tile_axes), lax.axis_size(tile_axes)
    quarter = height // 4
    low, high = quarter - RADIUS, height - quarter + RADIUS

    upper_mid = ringed(center[low:high], "gz", -1)

    codes = (class_map[0] + 1).astype(jnp.bfloat16).reshape(-1, channels, breadth)
    top = jnp.concatenate([center[:RADIUS], codes[:1]])
    bottom = jnp.concatenate([center[-RADIUS:], codes[-1:]])
    nothing = jnp.zeros_like(top)
    before = jnp.where(tile > 0, ringed(bottom, tile_axes, 1), nothing)
    after = jnp.where(tile < tiles - 1, ringed(top, tile_axes, -1), nothing)
    own_codes = jnp.concatenate(
        [before[RADIUS, -STEPS:], codes.reshape(height, breadth), after[RADIUS, :STEPS]]
    )
    spare = -own_codes.shape[0] % channels
    packed = jnp.pad(own_codes, ((0, spare), (0, 0))).reshape(-1, channels, breadth)
    upper_out = ringed(
        jnp.concatenate([before[:RADIUS], center[:low], center[high:], after[:RADIUS], packed]),
        "gz",
        -1,
    )
    outer = low + RADIUS
    upper_codes = upper_out[2 * outer :].reshape(-1, breadth)[: own_codes.shape[0]]

    def own_at(row):
        if row < 0:
            return 1, row + RADIUS
        return (0, row) if row < height else (2, row - height)

    def upper_at(row):
        if low <= row < high:
            return 0, row - low
        return (1, row + RADIUS) if row < low else (1, row - high + outer)

    sound = jnp.pad(valid.astype(jnp.float32), ((1, 1), (1, 1)))
    near = lax.dynamic_slice(sound, (section, tile), (3, 3))
    links = near[:-1] * near[1:]
    by_row = jnp.concatenate(
        [
            jnp.broadcast_to(links[:, k : k + 1], (2, count))
            for k, count in enumerate((STEPS, height, STEPS))
        ],
        axis=1,
    )

    def own_links(begin, count):
        return by_row[1][None, begin : begin + count, None]

    live = jnp.where(section < sections - 1, 1.0, 0.0)[None]
    middle_rows = range(quarter, height - quarter, BLOCK)
    middle = flows(live, [center], [upper_mid], own_at, upper_at, middle_rows)
    by_mid = own_links(quarter + STEPS, height // 2)
    sent_mid = messages(middle, by_mid, section)
    n_mid = 6 * middle.shape[1]
    below_mid = ringed(jnp.concatenate([sent_mid[0].reshape(n_mid, breadth), own_codes]), "gz", 1)
    before_mid = ringed(sent_mid[1], "gz", 2)
    above_mid = ringed(sent_mid[2], "gz", -1)
    outer_rows = [*range(0, quarter, BLOCK), *range(height - quarter, height, BLOCK)]
    outside = flows(
        live, [center, before, after], [upper_mid, upper_out], own_at, upper_at, outer_rows
    )

    head, tail = outside[:, :quarter], outside[:, quarter:]
    head = jnp.concatenate([ringed(tail[:, -STEPS:], tile_axes, 1), head], axis=1)
    tail = jnp.concatenate([tail, ringed(outside[:, :STEPS], tile_axes, -1)], axis=1)
    edge_rows = jnp.concatenate([head, tail], axis=1)
    first_tail = head.shape[1]
    by_edge = jnp.concatenate(
        [own_links(0, first_tail), own_links(height + 2 * STEPS - first_tail, first_tail)], axis=1
    )
    sent_out = messages(edge_rows, by_edge, section)
    below_out = ringed(sent_out[0], "gz", 1)
    before_out = ringed(sent_out[1], "gz", 2)
    above_out = ringed(sent_out[2], "gz", -1)

    def whole(inner, outer):
        return jnp.concatenate([outer[:, :first_tail], inner, outer[:, first_tail:]], axis=1)

    both = whole(middle, edge_rows)
    fwd, ahd = both[:2], both[2:]
    from_below = whole(below_mid[:n_mid].reshape(6, -1, breadth), below_out)
    from_before = whole(before_mid, before_out)
    from_above = whole(above_mid, above_out)
    gain_below, pri = joined(from_below), from_below[4:].astype(jnp.float32)
    bwd = pri - gain_below
    part_before = from_before[4:].astype(jnp.float32)
    part_above = from_above[:2].astype(jnp.float32)
    earlier = jnp.where(section > 1, joined(from_before), 0.0)
    if sections <= 4:
        earlier = earlier + jnp.where(section > 2, joined(from_above[2:]), 0.0)
    forward = fwd[:, STEPS:-STEPS]

    def stiff_of(code):
        levels = jnp.arange(stiffness.shape[0], dtype=jnp.float32)[:, None, None] + 1.0
        code = code.astype(jnp.float32)
        field = jnp.sum(jnp.where(code[None] == levels, stiffness[:, None, None], 0.0), axis=0)
        return field, code > 0.0

    stiff, inside = stiff_of(own_codes)
    stiff_up, inside_up = stiff_of(upper_codes)
    stiff_down, inside_down = stiff_of(below_mid[n_mid:])

    below, here = by_row[0][None, :, None], by_row[1][None, :, None]

    gain = here * (fwd - ahd)
    start = 0.5 * (earlier + gain_below)
    part = pair_part(0.5 * gain, here, fwd, ahd)
    part_below = pair_part(0.5 * gain_below, below, pri, bwd)

    start_up = start + 0.5 * gain
    start_down = start - 0.5 * gain_below
    first = relaxed(start, stiff, inside) + trim(1, part - part_below)
    first_up = relaxed(trim(1, start_up), trim(1, stiff_up), trim(1, inside_up)) + trim(
        2, part_above - part
    )
    first_down = relaxed(
        trim(1, start_down), trim(1, stiff_down), trim(1, inside_down)
    ) + trim(2, part_below - part_before)
    mid = trim(1, first)
    up = [trim(2, x) for x in (here, fwd, ahd)]
    down = [trim(2, x) for x in (below, pri, bwd)]
    second = relaxed(first, trim(1, stiff), trim(1, inside))
    second = second + pair_part(first_up - mid, *up) - pair_part(mid - first_down, *down)
    change = (trim(1, second) - trim(3, start)).astype(jnp.bfloat16)
    last_up = trim(3, start_up) + ringed(change, "gz", -1).astype(jnp.float32)
    last_down = trim(3, start_down) + ringed(change, "gz", 1).astype(jnp.float32)
    mid = trim(1, second)
    up, down = ([trim(1, x) for x in fields] for fields in (up, down))
    third = relaxed(second, trim(2, stiff), trim(2, inside))
    third = third + pair_part(last_up - mid, *up) - pair_part(mid - last_down, *down)
    return (third[None], forward[None])


def solution(mesh):
    placed = (
        P(("groups", "gz"), None, tile_axes, None),
        P(("groups", "gz"), tile_axes, None),
        P(),
        P("groups", None),
    )
    return jax.shard_map(
        on_device,
        mesh=mesh,
        in_specs=placed,
        out_specs=(P(("groups", "gz"), None, tile_axes, None),) * 2,
        check_vma=False,
    )
```

```python
import functools

import jax
import jax.numpy as jnp
from jax import lax
from jax.experimental import pallas as pl
from jax.experimental.pallas import tpu as pltpu
from jax.sharding import PartitionSpec as P

RADIUS = 6
STEPS = 3
score_scale = 0.25
step_size = 0.1
saturation = 2.0
tile_axes = ("xy", "col")


def ringed(value, axis, steps):
    count = lax.axis_size(axis)
    return lax.ppermute(value, axis, [(i, (i + steps) % count) for i in range(count)])


BLOCK = 4
SPAN = BLOCK + 2 * RADIUS
GROUP = 32
LOG2E = 1.4426950408889634
MASKED = -1e30


def flow_kernel(
    early_rows, late_rows, n_early, live_ref, *refs
):
    n_in = n_early + 1 + max(i for i, _ in late_rows)
    ins, out_ref = refs[:n_in], refs[n_in]
    t_ref, bias_ref, o_ref, s0_ref, s1_ref, s2_ref, s3_ref, w_ref = refs[n_in + 1 :]
    channels, breadth = ins[0].shape[1:]
    groups = 1
    steps = breadth // BLOCK // 2
    wide = t_ref.shape[3]
    lane = lax.broadcasted_iota(jnp.int32, (8, 128), 1)
    sub = lax.broadcasted_iota(jnp.int32, (8, 128), 0)
    qc = lane // GROUP
    qr = lane % GROUP // (GROUP // BLOCK)
    col_ok = []
    for half in range(2):
        kc = sub + 8 * half
        col_ok.append((kc >= qc) & (kc <= qc + 2 * RADIUS))
    edge = [k for k in range(SPAN) if k < BLOCK - 1 or k > 2 * RADIUS]
    for n, kr in enumerate(edge):
        row_ok = (qr <= kr) & (kr <= qr + 2 * RADIUS)
        for half in range(2):
            bias_ref[2 * n + half] = jnp.where(row_ok & col_ok[half], 0.0, MASKED)
    place = jnp.where(
        lax.broadcasted_iota(jnp.int32, (wide, breadth), 0)
        == lax.broadcasted_iota(jnp.int32, (wide, breadth), 1) + RADIUS,
        1.0,
        0.0,
    ).astype(jnp.bfloat16)
    per = GROUP // BLOCK
    for side, (offset, table) in enumerate(((0, early_rows), (n_early, late_rows))):
        for g in range(groups):
            for kr in range(0, SPAN, 2):
                pieces = []
                for k in range(2):
                    for b in range(per):
                        which, row = table[SPAN * b + kr + k]
                        pieces.append(ins[offset + which][row])
                flat = jnp.concatenate(pieces, axis=0)
                out = lax.dot_general(
                    place, flat, (((1,), (1,)), ((), ())), preferred_element_type=jnp.float32
                )
                t_ref[side, g, kr] = out[:, :128]
                t_ref[side, g, kr + 1] = out[:, 128:]

    diagonal = lane // channels == sub
    zero_b = jnp.zeros((16, 128), jnp.bfloat16)
    for side in range(2):

        def tiles_of(i):
            tiles = []
            for k in range(2):
                g = 0
                base = i * BLOCK + k * (breadth // 2)
                tiles.append((g, base))
            return tiles

        def score(i, s_ref):
            tiles = tiles_of(i)
            keys = []
            for kr in range(SPAN):
                keys.append(
                    jnp.concatenate(
                        [t_ref[1 - side, g, kr, pl.ds(base, SPAN), :] for g, base in tiles], axis=1
                    ).astype(jnp.bfloat16)
                )
            keys = jnp.concatenate(keys, axis=0)
            parts = []
            for k, (g, base) in enumerate(tiles):
                for c in range(BLOCK):
                    for r in range(0, BLOCK, 2):
                        pair = [
                            jnp.where(
                                diagonal,
                                t_ref[side, g, RADIUS + r + m, pl.ds(base + RADIUS + c, 1), :],
                                0.0,
                            )
                            for m in range(2)
                        ]
                        sel = jnp.concatenate(pair, axis=0).astype(jnp.bfloat16)
                        parts.append(
                            jnp.concatenate([sel, zero_b] if k == 0 else [zero_b, sel], axis=1)
                        )
            queries = jnp.concatenate(parts, axis=0)
            s_ref[...] = lax.dot_general(
                keys, queries, (((1,), (1,)), ((), ())), preferred_element_type=jnp.float32
            )

        def settle(i, s_ref):
            for k, (g, base) in enumerate(tiles_of(i)):
                s = {}
                for kr in range(SPAN):
                    for half in range(2):
                        s[kr, half] = s_ref[
                            SPAN * kr + 8 * half : SPAN * kr + 8 * half + 8, 128 * k : 128 * k + 128
                        ]
                for n, kr in enumerate(edge):
                    for half in range(2):
                        s[kr, half] = s[kr, half] + bias_ref[2 * n + half]
                peak = []
                for half in range(2):
                    inner = functools.reduce(
                        jnp.maximum, [s[kr, half] for kr in range(SPAN) if kr not in edge]
                    )
                    inner = jnp.where(col_ok[half], inner, MASKED)
                    peak.append(
                        functools.reduce(jnp.maximum, [s[kr, half] for kr in edge] + [inner])
                    )
                top = jnp.max(jnp.maximum(peak[0], peak[1]), axis=0, keepdims=True)
                top = jnp.broadcast_to(top, (8, 128))
                total, slope = [], []
                for half in range(2):
                    acc = None
                    mom = None
                    for kr in reversed(range(SPAN)):
                        w = jnp.exp2((s[kr, half] - top) * (LOG2E * score_scale))
                        acc = w if acc is None else acc + w
                        if kr > 0:
                            mom = acc if mom is None else mom + acc
                    total.append(jnp.where(col_ok[half], acc, 0.0))
                    slope.append(jnp.where(col_ok[half], mom, 0.0))
                both = total[0] + total[1]
                den = jnp.sum(both, axis=0, keepdims=True)
                row_sum = jnp.sum(slope[0] + slope[1], axis=0, keepdims=True)
                col_sum = jnp.sum(
                    both * sub.astype(jnp.float32) + 8.0 * total[1], axis=0, keepdims=True
                )
                fr = row_sum / den - (qr[0:1] + RADIUS).astype(jnp.float32)
                fc = col_sum / den - (qc[0:1] + RADIUS).astype(jnp.float32)
                both_f = jnp.concatenate([fr, fc], axis=0)
                for c in range(BLOCK):
                    r = both_f if c == 0 else pltpu.roll(both_f, 128 - GROUP * c, 1)
                    o_ref[side, 0, g, pl.ds(base + c, 1), :] = r[0:1]
                    o_ref[side, 1, g, pl.ds(base + c, 1), :] = r[1:2]

        def step(j, carry):
            last = steps - 1
            score(4 * j + 2, s2_ref)
            settle(4 * j, s0_ref)
            score(4 * j + 3, s3_ref)
            settle(4 * j + 1, s1_ref)
            score(jnp.minimum(4 * j + 4, last), s0_ref)
            settle(4 * j + 2, s2_ref)
            score(jnp.minimum(4 * j + 5, last), s1_ref)
            settle(4 * j + 3, s3_ref)
            return carry

        score(0, s0_ref)
        score(1, s1_ref)
        lax.fori_loop(0, steps // 4, step, 0)
    live = live_ref[0]
    for side in range(2):
        for comp in range(2):
            turned = jnp.transpose(o_ref[side, comp, 0], (1, 0)) * live
            for t in range(breadth // 128):
                for r in range(BLOCK):
                    w_ref[side, comp, t, pl.ds(r, per, stride=BLOCK), :] = turned[
                        per * r : per * r + per, 128 * t : 128 * t + 128
                    ]
                out_ref[2 * side + comp, :, 128 * t : 128 * t + 128] = w_ref[side, comp, t]


def flows(live, early, late, early_at, late_at, starts):
    _, breadth = early[0].shape[1:]
    wide = breadth + 16
    tables = [
        [at(start - RADIUS + k) for start in starts for k in range(SPAN)]
        for at in (early_at, late_at)
    ]
    cells = GROUP * breadth
    return pl.pallas_call(
        functools.partial(flow_kernel, *tables, len(early)),
        out_shape=jax.ShapeDtypeStruct((4, GROUP, breadth), jnp.float32),
        in_specs=[pl.BlockSpec(memory_space=pltpu.SMEM)]
        + [pl.BlockSpec(memory_space=pltpu.VMEM)] * (len(early) + len(late)),
        out_specs=pl.BlockSpec(memory_space=pltpu.VMEM),
        scratch_shapes=[
            pltpu.VMEM((2, 1, SPAN, wide, 128), jnp.float32),
            pltpu.VMEM((12, 8, 128), jnp.float32),
            pltpu.VMEM((2, 2, 1, breadth, 128), jnp.float32),
        ]
        + [pltpu.VMEM((SPAN * SPAN, 256), jnp.float32)] * 4
        + [pltpu.VMEM((2, 2, breadth // 128, GROUP, 128), jnp.float32)],
        compiler_params=pltpu.CompilerParams(vmem_limit_bytes=24 * 2**20),
        cost_estimate=pl.CostEstimate(
            flops=2 * cells * SPAN * SPAN * 2 * 256, bytes_accessed=2**22, transcendentals=2 * cells * SPAN * SPAN
        ),
        name="flows",
    )(live, *early, *late)


def spring(vector):
    squares = jnp.sum(vector * vector, axis=0, keepdims=True)
    return vector / jnp.sqrt(1.0 + squares / (saturation * saturation))


def pair_part(apart, here, forward, ahead):
    return step_size * here * (spring(apart - forward) - spring(-apart - ahead))


def split(value):
    high = lax.reduce_precision(value, 8, 7)
    return [high.astype(jnp.bfloat16), (value - high).astype(jnp.bfloat16)]


def running(gain, section):
    count = lax.axis_size("gz")
    reach = 1
    while count > 4 and reach < count - 2:
        more = jnp.where(section >= reach, ringed(gain, "gz", reach), 0.0)
        gain, reach = gain + more, 2 * reach
    return gain


def messages(flow, here, section):
    forward, ahead = flow[:2], flow[2:]
    gain = here * (forward - ahead)
    part = pair_part(0.5 * gain, here, forward, ahead).astype(jnp.bfloat16)
    halves = split(gain)
    to_next = jnp.concatenate([*halves, forward.astype(jnp.bfloat16)])
    to_second = jnp.concatenate([*split(running(gain, section)), part])
    return to_next, to_second, jnp.concatenate([part, *halves])


FRAME = 8


def spring_pair(row, col):
    length = jnp.sqrt(1.0 + (row * row + col * col) / (saturation * saturation))
    return row / length, col / length


def pair_pull(apart, here, forward, ahead):
    one = spring_pair(*[a - f for a, f in zip(apart, forward)])
    two = spring_pair(*[-a - b for a, b in zip(apart, ahead)])
    return [step_size * here * (x - y) for x, y in zip(one, two)]


def beside(value, edges):
    first, last = edges
    rows, cols = value.shape
    return (
        pltpu.roll(value, rows - 1, 0),
        pltpu.roll(value, 1, 0),
        jnp.where(last, 0.0, pltpu.roll(value, cols - 1, 1)),
        jnp.where(first, 0.0, pltpu.roll(value, 1, 1)),
    )


def springs_of(stiff, edges):
    return [0.5 * (stiff + s) for s in beside(stiff, edges)]


def eased(u, weights, inside, edges):
    out = []
    for part in u:
        total = 0.0
        for w, n in zip(weights, beside(part, edges)):
            total = total + w * (part - n)
        out.append(jnp.where(inside, part - step_size * total, 0.0))
    return out


def early_kernel(
    links_ref, stiffness_ref, depth_ref, middle_ref, edge_ref, below_mid_ref, below_out_ref, before_mid_ref,
    before_out_ref, above_mid_ref, above_out_ref, own_ref, upper_ref, lower_ref, change_ref, state_ref, frame_ref
):
    rows, cols = state_ref.shape[1:]
    height, thick = rows - 2 * FRAME, middle_ref.shape[1]
    side = edge_ref.shape[1] // 2
    top, low = FRAME - STEPS, FRAME + (height - thick) // 2

    def framed(mid, out):
        frame_ref[top : top + side] = out[:side]
        frame_ref[low : low + thick] = mid
        frame_ref[low + thick : low + thick + side] = out[side:]
        return frame_ref[...]

    def fields(mid_ref, out_ref, at):
        return [
            framed(mid_ref[i].astype(jnp.float32), out_ref[i].astype(jnp.float32))
            for i in range(at, at + 2)
        ]

    def coded(ref):
        frame_ref[...] = jnp.zeros((rows, cols), jnp.float32)
        frame_ref[top : top + height + 2 * STEPS] = ref[...].astype(jnp.float32)[: height + 2 * STEPS]
        code = frame_ref[...]
        stiff = jnp.zeros((rows, cols), jnp.float32)
        for k in range(stiffness_ref.shape[0]):
            stiff = jnp.where(code == k + 1.0, stiffness_ref[k], stiff)
        return stiff, code > 0.0

    row = lax.broadcasted_iota(jnp.int32, (rows, cols), 0)
    col = lax.broadcasted_iota(jnp.int32, (rows, cols), 1)
    edges = (col == 0, col == cols - 1)

    def linked(k):
        outer = jnp.where(row < FRAME, links_ref[k, 0], links_ref[k, 2])
        return jnp.where((row >= FRAME) & (row < FRAME + height), links_ref[k, 1], outer)

    below, here = linked(0), linked(1)
    stiff, inside = coded(own_ref)
    stiff_up, inside_up = coded(upper_ref)
    stiff_down, inside_down = coded(lower_ref)
    fwd, ahd = fields(middle_ref, edge_ref, 0), fields(middle_ref, edge_ref, 2)
    gain = [here * (f - a) for f, a in zip(fwd, ahd)]
    high, rest = fields(below_mid_ref, below_out_ref, 0), fields(below_mid_ref, below_out_ref, 2)
    gain_below = [h + r for h, r in zip(high, rest)]
    pri = fields(below_mid_ref, below_out_ref, 4)
    bwd = [p - g for p, g in zip(pri, gain_below)]
    high, rest = fields(before_mid_ref, before_out_ref, 0), fields(before_mid_ref, before_out_ref, 2)
    far = [jnp.where(depth_ref[0] > 1, h + r, 0.0) for h, r in zip(high, rest)]
    part_before = fields(before_mid_ref, before_out_ref, 4)
    part_above = fields(above_mid_ref, above_out_ref, 0)
    if above_mid_ref.shape[0] > 2:
        high, rest = fields(above_mid_ref, above_out_ref, 2), fields(above_mid_ref, above_out_ref, 4)
        far = [f + jnp.where(depth_ref[0] > 2, h + r, 0.0) for f, h, r in zip(far, high, rest)]

    start = [0.5 * (f + g) for f, g in zip(far, gain_below)]
    start_up = [s + 0.5 * g for s, g in zip(start, gain)]
    start_down = [s - 0.5 * g for s, g in zip(start, gain_below)]
    part = pair_pull([0.5 * g for g in gain], here, fwd, ahd)
    part_below = pair_pull([0.5 * g for g in gain_below], below, pri, bwd)

    weights = springs_of(stiff, edges)
    first = eased(start, weights, inside, edges)
    first = [u + p - q for u, p, q in zip(first, part, part_below)]
    first_up = eased(start_up, springs_of(stiff_up, edges), inside_up, edges)
    first_up = [u + p - q for u, p, q in zip(first_up, part_above, part)]
    first_down = eased(start_down, springs_of(stiff_down, edges), inside_down, edges)
    first_down = [u + p - q for u, p, q in zip(first_down, part_below, part_before)]
    pull = pair_pull([a - b for a, b in zip(first_up, first)], here, fwd, ahd)
    push = pair_pull([a - b for a, b in zip(first, first_down)], below, pri, bwd)
    second = [
        u + p - q for u, p, q in zip(eased(first, weights, inside, edges), pull, push)
    ]
    for i in range(2):
        change_ref[i] = (second[i] - start[i])[FRAME : FRAME + height].astype(jnp.bfloat16)
    for i, value in enumerate([*second, *start_up, *start_down, *fwd, *ahd, *pri, *bwd, here, below, stiff]):
        state_ref[i] = value


def late_kernel(up_ref, down_ref, state_ref, out_ref):
    rows, cols = state_ref.shape[1:]
    height = rows - 2 * FRAME
    body = slice(FRAME, FRAME + height)
    col = lax.broadcasted_iota(jnp.int32, (rows, cols), 1)
    edges = (col == 0, col == cols - 1)
    second = [state_ref[i] for i in range(2)]
    stiff = state_ref[16]
    third = eased(second, springs_of(stiff, edges), stiff > 0.0, edges)

    def two(at):
        return [state_ref[at + i, body, :] for i in range(2)]

    mid = two(0)
    up = [a + up_ref[i].astype(jnp.float32) - m for i, (a, m) in enumerate(zip(two(2), mid))]
    down = [m - a - down_ref[i].astype(jnp.float32) for i, (a, m) in enumerate(zip(two(4), mid))]
    pull = pair_pull(up, state_ref[14, body, :], two(6), two(8))
    push = pair_pull(down, state_ref[15, body, :], two(10), two(12))
    for i in range(2):
        out_ref[i] = third[i][body] + pull[i] - push[i]


def relaxation(change_shape, links, stiffness, depth, arrays):
    height, breadth = change_shape[1:]
    vmem, smem = pl.BlockSpec(memory_space=pltpu.VMEM), pl.BlockSpec(memory_space=pltpu.SMEM)
    change, state = pl.pallas_call(
        early_kernel,
        out_shape=(
            jax.ShapeDtypeStruct(change_shape, jnp.bfloat16),
            jax.ShapeDtypeStruct((17, height + 2 * FRAME, breadth), jnp.float32),
        ),
        in_specs=[smem] * 3 + [vmem] * len(arrays),
        out_specs=(vmem, vmem),
        scratch_shapes=[pltpu.VMEM((height + 2 * FRAME, breadth), jnp.float32)],
        compiler_params=pltpu.CompilerParams(vmem_limit_bytes=16 * 2**20),
        cost_estimate=pl.CostEstimate(flops=2**23, bytes_accessed=2**21, transcendentals=2**16),
        name="early_steps",
    )(links, stiffness, depth, *arrays)
    up, down = ringed(change, "gz", -1), ringed(change, "gz", 1)
    return pl.pallas_call(
        late_kernel,
        out_shape=jax.ShapeDtypeStruct(change_shape, jnp.float32),
        in_specs=[vmem] * 3,
        out_specs=vmem,
        compiler_params=pltpu.CompilerParams(vmem_limit_bytes=16 * 2**20),
        cost_estimate=pl.CostEstimate(flops=2**22, bytes_accessed=2**21, transcendentals=2**15),
        name="last_step",
    )(up, down, state)


def whole_device(features, class_map, stiffness, valid):
    center = jnp.transpose(features[0], (1, 0, 2))
    height, channels, breadth = center.shape
    section, sections = lax.axis_index("gz"), lax.axis_size("gz")
    tile, tiles = lax.axis_index(tile_axes), lax.axis_size(tile_axes)
    quarter = height // 4
    low, high = quarter - RADIUS, height - quarter + RADIUS

    upper_mid = ringed(center[low:high], "gz", -1)

    codes = (class_map[0] + 1).astype(jnp.bfloat16).reshape(-1, channels, breadth)
    top = jnp.concatenate([center[:RADIUS], codes[:1]])
    bottom = jnp.concatenate([center[-RADIUS:], codes[-1:]])
    nothing = jnp.zeros_like(top)
    before = jnp.where(tile > 0, ringed(bottom, tile_axes, 1), nothing)
    after = jnp.where(tile < tiles - 1, ringed(top, tile_axes, -1), nothing)
    own_codes = jnp.concatenate(
        [before[RADIUS, -STEPS:], codes.reshape(height, breadth), after[RADIUS, :STEPS]]
    )
    spare = -own_codes.shape[0] % channels
    packed = jnp.pad(own_codes, ((0, spare), (0, 0))).reshape(-1, channels, breadth)
    upper_out = ringed(
        jnp.concatenate([before[:RADIUS], center[:low], center[high:], after[:RADIUS], packed]),
        "gz",
        -1,
    )
    outer = low + RADIUS
    upper_codes = upper_out[2 * outer :].reshape(-1, breadth)[: own_codes.shape[0]]

    def own_at(row):
        if row < 0:
            return 1, row + RADIUS
        return (0, row) if row < height else (2, row - height)

    def upper_at(row):
        if low <= row < high:
            return 0, row - low
        return (1, row + RADIUS) if row < low else (1, row - high + outer)

    sound = jnp.pad(valid.astype(jnp.float32), ((1, 1), (1, 1)))
    near = lax.dynamic_slice(sound, (section, tile), (3, 3))
    links = near[:-1] * near[1:]
    by_row = jnp.concatenate(
        [
            jnp.broadcast_to(links[:, k : k + 1], (2, count))
            for k, count in enumerate((STEPS, height, STEPS))
        ],
        axis=1,
    )

    def own_links(begin, count):
        return by_row[1][None, begin : begin + count, None]

    live = jnp.where(section < sections - 1, 1.0, 0.0)[None]
    middle_rows = range(quarter, height - quarter, BLOCK)
    middle = flows(live, [center], [upper_mid], own_at, upper_at, middle_rows)
    by_mid = own_links(quarter + STEPS, height // 2)
    sent_mid = messages(middle, by_mid, section)
    n_mid = 6 * middle.shape[1]
    below_mid = ringed(jnp.concatenate([sent_mid[0].reshape(n_mid, breadth), own_codes]), "gz", 1)
    before_mid = ringed(sent_mid[1], "gz", 2)
    above_mid = ringed(sent_mid[2], "gz", -1)
    outer_rows = [*range(0, quarter, BLOCK), *range(height - quarter, height, BLOCK)]
    outside = flows(
        live, [center, before, after], [upper_mid, upper_out], own_at, upper_at, outer_rows
    )

    head, tail = outside[:, :quarter], outside[:, quarter:]
    head = jnp.concatenate([ringed(tail[:, -STEPS:], tile_axes, 1), head], axis=1)
    tail = jnp.concatenate([tail, ringed(outside[:, :STEPS], tile_axes, -1)], axis=1)
    edge_rows = jnp.concatenate([head, tail], axis=1)
    first_tail = head.shape[1]
    by_edge = jnp.concatenate(
        [own_links(0, first_tail), own_links(height + 2 * STEPS - first_tail, first_tail)], axis=1
    )
    sent_out = messages(edge_rows, by_edge, section)
    below_out = ringed(sent_out[0], "gz", 1)
    before_out = ringed(sent_out[1], "gz", 2)
    above_out = ringed(sent_out[2], "gz", -1)

    forward = jnp.concatenate(
        [outside[:2, :quarter], middle[:2], outside[:2, quarter:]], axis=1
    )
    arrays = [
        middle,
        edge_rows,
        below_mid[:n_mid].reshape(6, -1, breadth),
        below_out,
        before_mid,
        before_out,
        above_mid,
        above_out,
        own_codes,
        upper_codes,
        below_mid[n_mid:],
    ]
    third = relaxation((2, height, breadth), links, stiffness, section[None], arrays)
    return (third[None], forward[None])


def solution(mesh):
    placed = (
        P(("groups", "gz"), None, tile_axes, None),
        P(("groups", "gz"), tile_axes, None),
        P(),
        P("groups", None),
    )
    return jax.shard_map(
        whole_device,
        mesh=mesh,
        in_specs=placed,
        out_specs=(P(("groups", "gz"), None, tile_axes, None),) * 2,
        check_vma=False,
    )
```

```python
import functools

import jax
import jax.numpy as jnp
from jax import lax
from jax.experimental import pallas as pl
from jax.experimental.pallas import tpu as pltpu
from jax.sharding import PartitionSpec as P

RADIUS = 6
STEPS = 3
score_scale = 0.25
step_size = 0.1
saturation = 2.0
tile_axes = ("xy", "col")


def ringed(value, axis, steps):
    count = lax.axis_size(axis)
    return lax.ppermute(value, axis, [(i, (i + steps) % count) for i in range(count)])


BLOCK = 4
SPAN = BLOCK + 2 * RADIUS
GROUP = 32
LOG2E = 1.4426950408889634
MASKED = -1e30


def flow_kernel(
    early_rows, late_rows, n_early, live_ref, *refs
):
    n_in = n_early + 1 + max(i for i, _ in late_rows)
    ins, out_ref = refs[:n_in], refs[n_in]
    t_ref, bias_ref, o_ref, s0_ref, s1_ref, s2_ref, s3_ref, w_ref = refs[n_in + 1 :]
    channels, breadth = ins[0].shape[1:]
    groups = 1
    steps = breadth // BLOCK // 2
    wide = t_ref.shape[3]
    lane = lax.broadcasted_iota(jnp.int32, (8, 128), 1)
    sub = lax.broadcasted_iota(jnp.int32, (8, 128), 0)
    qc = lane // GROUP
    qr = lane % GROUP // (GROUP // BLOCK)
    col_ok = []
    for half in range(2):
        kc = sub + 8 * half
        col_ok.append((kc >= qc) & (kc <= qc + 2 * RADIUS))
    edge = [k for k in range(SPAN) if k < BLOCK - 1 or k > 2 * RADIUS]
    for n, kr in enumerate(edge):
        row_ok = (qr <= kr) & (kr <= qr + 2 * RADIUS)
        for half in range(2):
            bias_ref[2 * n + half] = jnp.where(row_ok & col_ok[half], 0.0, MASKED)
    place = jnp.where(
        lax.broadcasted_iota(jnp.int32, (wide, breadth), 0)
        == lax.broadcasted_iota(jnp.int32, (wide, breadth), 1) + RADIUS,
        1.0,
        0.0,
    ).astype(jnp.bfloat16)
    per = GROUP // BLOCK
    for side, (offset, table) in enumerate(((0, early_rows), (n_early, late_rows))):
        for g in range(groups):
            for kr in range(0, SPAN, 2):
                pieces = []
                for k in range(2):
                    for b in range(per):
                        which, row = table[SPAN * b + kr + k]
                        pieces.append(ins[offset + which][row])
                flat = jnp.concatenate(pieces, axis=0)
                out = lax.dot_general(
                    place, flat, (((1,), (1,)), ((), ())), preferred_element_type=jnp.float32
                )
                t_ref[side, g, kr] = out[:, :128]
                t_ref[side, g, kr + 1] = out[:, 128:]

    diagonal = lane // channels == sub
    zero_b = jnp.zeros((16, 128), jnp.bfloat16)
    for side in range(2):

        def tiles_of(i):
            tiles = []
            for k in range(2):
                g = 0
                base = i * BLOCK + k * (breadth // 2)
                tiles.append((g, base))
            return tiles

        def score(i, s_ref):
            tiles = tiles_of(i)
            keys = []
            for kr in range(SPAN):
                keys.append(
                    jnp.concatenate(
                        [t_ref[1 - side, g, kr, pl.ds(base, SPAN), :] for g, base in tiles], axis=1
                    ).astype(jnp.bfloat16)
                )
            keys = jnp.concatenate(keys, axis=0)
            parts = []
            for k, (g, base) in enumerate(tiles):
                for c in range(BLOCK):
                    for r in range(0, BLOCK, 2):
                        pair = [
                            jnp.where(
                                diagonal,
                                t_ref[side, g, RADIUS + r + m, pl.ds(base + RADIUS + c, 1), :],
                                0.0,
                            )
                            for m in range(2)
                        ]
                        sel = jnp.concatenate(pair, axis=0).astype(jnp.bfloat16)
                        parts.append(
                            jnp.concatenate([sel, zero_b] if k == 0 else [zero_b, sel], axis=1)
                        )
            queries = jnp.concatenate(parts, axis=0)
            s_ref[...] = lax.dot_general(
                keys, queries, (((1,), (1,)), ((), ())), preferred_element_type=jnp.float32
            )

        def settle(i, s_ref):
            for k, (g, base) in enumerate(tiles_of(i)):
                s = {}
                for kr in range(SPAN):
                    for half in range(2):
                        s[kr, half] = s_ref[
                            SPAN * kr + 8 * half : SPAN * kr + 8 * half + 8, 128 * k : 128 * k + 128
                        ]
                for n, kr in enumerate(edge):
                    for half in range(2):
                        s[kr, half] = s[kr, half] + bias_ref[2 * n + half]
                peak = []
                for half in range(2):
                    inner = functools.reduce(
                        jnp.maximum, [s[kr, half] for kr in range(SPAN) if kr not in edge]
                    )
                    inner = jnp.where(col_ok[half], inner, MASKED)
                    peak.append(
                        functools.reduce(jnp.maximum, [s[kr, half] for kr in edge] + [inner])
                    )
                top = jnp.max(jnp.maximum(peak[0], peak[1]), axis=0, keepdims=True)
                top = jnp.broadcast_to(top, (8, 128))
                total, slope = [], []
                for half in range(2):
                    acc = None
                    mom = None
                    for kr in reversed(range(SPAN)):
                        w = jnp.exp2((s[kr, half] - top) * (LOG2E * score_scale))
                        acc = w if acc is None else acc + w
                        if kr > 0:
                            mom = acc if mom is None else mom + acc
                    total.append(jnp.where(col_ok[half], acc, 0.0))
                    slope.append(jnp.where(col_ok[half], mom, 0.0))
                both = total[0] + total[1]
                den = jnp.sum(both, axis=0, keepdims=True)
                row_sum = jnp.sum(slope[0] + slope[1], axis=0, keepdims=True)
                col_sum = jnp.sum(
                    both * sub.astype(jnp.float32) + 8.0 * total[1], axis=0, keepdims=True
                )
                fr = row_sum / den - (qr[0:1] + RADIUS).astype(jnp.float32)
                fc = col_sum / den - (qc[0:1] + RADIUS).astype(jnp.float32)
                both_f = jnp.concatenate([fr, fc], axis=0)
                for c in range(BLOCK):
                    r = both_f if c == 0 else pltpu.roll(both_f, 128 - GROUP * c, 1)
                    o_ref[side, 0, g, pl.ds(base + c, 1), :] = r[0:1]
                    o_ref[side, 1, g, pl.ds(base + c, 1), :] = r[1:2]

        def step(j, carry):
            last = steps - 1
            score(4 * j + 2, s2_ref)
            settle(4 * j, s0_ref)
            score(4 * j + 3, s3_ref)
            settle(4 * j + 1, s1_ref)
            score(jnp.minimum(4 * j + 4, last), s0_ref)
            settle(4 * j + 2, s2_ref)
            score(jnp.minimum(4 * j + 5, last), s1_ref)
            settle(4 * j + 3, s3_ref)
            return carry

        score(0, s0_ref)
        score(1, s1_ref)
        lax.fori_loop(0, steps // 4, step, 0)
    live = live_ref[0]
    for side in range(2):
        for comp in range(2):
            turned = jnp.transpose(o_ref[side, comp, 0], (1, 0)) * live
            for t in range(breadth // 128):
                for r in range(BLOCK):
                    w_ref[side, comp, t, pl.ds(r, per, stride=BLOCK), :] = turned[
                        per * r : per * r + per, 128 * t : 128 * t + 128
                    ]
                out_ref[2 * side + comp, :, 128 * t : 128 * t + 128] = w_ref[side, comp, t]


def flows(live, early, late, early_at, late_at, starts):
    _, breadth = early[0].shape[1:]
    wide = breadth + 16
    tables = [
        [at(start - RADIUS + k) for start in starts for k in range(SPAN)]
        for at in (early_at, late_at)
    ]
    cells = GROUP * breadth
    return pl.pallas_call(
        functools.partial(flow_kernel, *tables, len(early)),
        out_shape=jax.ShapeDtypeStruct((4, GROUP, breadth), jnp.float32),
        in_specs=[pl.BlockSpec(memory_space=pltpu.SMEM)]
        + [pl.BlockSpec(memory_space=pltpu.VMEM)] * (len(early) + len(late)),
        out_specs=pl.BlockSpec(memory_space=pltpu.VMEM),
        scratch_shapes=[
            pltpu.VMEM((2, 1, SPAN, wide, 128), jnp.float32),
            pltpu.VMEM((12, 8, 128), jnp.float32),
            pltpu.VMEM((2, 2, 1, breadth, 128), jnp.float32),
        ]
        + [pltpu.VMEM((SPAN * SPAN, 256), jnp.float32)] * 4
        + [pltpu.VMEM((2, 2, breadth // 128, GROUP, 128), jnp.float32)],
        compiler_params=pltpu.CompilerParams(vmem_limit_bytes=24 * 2**20),
        cost_estimate=pl.CostEstimate(
            flops=2 * cells * SPAN * SPAN * 2 * 256, bytes_accessed=2**22, transcendentals=2 * cells * SPAN * SPAN
        ),
        name="flows",
    )(live, *early, *late)


def spring(vector):
    squares = jnp.sum(vector * vector, axis=0, keepdims=True)
    return vector / jnp.sqrt(1.0 + squares / (saturation * saturation))


def swapped(value, axis, parity):
    firsts = range(parity, lax.axis_size(axis) - 1, 2)
    pairs = [(i + k, i + 1 - k) for i in firsts for k in range(2)]
    return lax.ppermute(value, axis, pairs)


def pair_part(apart, here, forward, ahead):
    return step_size * here * (spring(apart - forward) - spring(-apart - ahead))


def split(value):
    high = lax.reduce_precision(value, 8, 7)
    return [high.astype(jnp.bfloat16), (value - high).astype(jnp.bfloat16)]


def running(gain, section):
    count = lax.axis_size("gz")
    reach = 1
    while count > 4 and reach < count - 2:
        more = jnp.where(section >= reach, ringed(gain, "gz", reach), 0.0)
        gain, reach = gain + more, 2 * reach
    return gain


def messages(flow, here, section):
    forward, ahead = flow[:2], flow[2:]
    gain = here * (forward - ahead)
    part = pair_part(0.5 * gain, here, forward, ahead).astype(jnp.bfloat16)
    halves = split(gain)
    to_next = jnp.concatenate([*halves, forward.astype(jnp.bfloat16)])
    to_second = jnp.concatenate([*split(running(gain, section)), part])
    return to_next, to_second, jnp.concatenate([part, *halves])


FRAME = 8


def spring_pair(row, col):
    inverse = lax.rsqrt(1.0 + (row * row + col * col) * (1.0 / (saturation * saturation)))
    return row * inverse, col * inverse


def pair_pull(apart, here, forward, ahead):
    one = spring_pair(*[a - f for a, f in zip(apart, forward)])
    two = spring_pair(*[-a - b for a, b in zip(apart, ahead)])
    return [step_size * here * (x - y) for x, y in zip(one, two)]


def beside(value, edges):
    first, last = edges
    rows, cols = value.shape
    return (
        pltpu.roll(value, rows - 1, 0),
        pltpu.roll(value, 1, 0),
        jnp.where(last, 0.0, pltpu.roll(value, cols - 1, 1)),
        jnp.where(first, 0.0, pltpu.roll(value, 1, 1)),
    )


def springs_of(stiff, edges):
    return [0.5 * (stiff + s) for s in beside(stiff, edges)]


def eased(u, weights, inside, edges):
    out = []
    for part in u:
        total = 0.0
        for w, n in zip(weights, beside(part, edges)):
            total = total + w * (part - n)
        out.append(jnp.where(inside, part - step_size * total, 0.0))
    return out


def early_kernel(
    deep, links_ref, stiffness_ref, depth_ref, middle_ref, edge_ref, below_mid_ref, below_out_ref, before_mid_ref,
    before_out_ref, above_mid_ref, above_out_ref, own_ref, upper_ref, lower_ref, change_ref, state_ref, frame_ref
):
    rows, cols = state_ref.shape[1:]
    height, thick = rows - 2 * FRAME, middle_ref.shape[1]
    side = edge_ref.shape[1] // 2
    top, low = FRAME - STEPS, FRAME + (height - thick) // 2

    def framed(mid, out):
        frame_ref[top : top + side] = out[:side]
        frame_ref[low : low + thick] = mid
        frame_ref[low + thick : low + thick + side] = out[side:]
        return frame_ref[...]

    def fields(mid_ref, out_ref, at):
        return [
            framed(mid_ref[i].astype(jnp.float32), out_ref[i].astype(jnp.float32))
            for i in range(at, at + 2)
        ]

    def coded(ref):
        frame_ref[...] = jnp.zeros((rows, cols), jnp.float32)
        frame_ref[top : top + height + 2 * STEPS] = ref[...].astype(jnp.float32)[: height + 2 * STEPS]
        code = frame_ref[...]
        stiff = jnp.zeros((rows, cols), jnp.float32)
        for k in range(stiffness_ref.shape[0]):
            stiff = jnp.where(code == k + 1.0, stiffness_ref[k], stiff)
        return stiff, code > 0.0

    row = lax.broadcasted_iota(jnp.int32, (rows, cols), 0)
    col = lax.broadcasted_iota(jnp.int32, (rows, cols), 1)
    edges = (col == 0, col == cols - 1)

    def linked(k):
        outer = jnp.where(row < FRAME, links_ref[k, 0], links_ref[k, 2])
        return jnp.where((row >= FRAME) & (row < FRAME + height), links_ref[k, 1], outer)

    below, here = linked(0), linked(1)
    stiff, inside = coded(own_ref)
    stiff_up, inside_up = coded(upper_ref)
    stiff_down, inside_down = coded(lower_ref)
    fwd, ahd = fields(middle_ref, edge_ref, 0), fields(middle_ref, edge_ref, 2)
    gain = [here * (f - a) for f, a in zip(fwd, ahd)]
    high, rest = fields(below_mid_ref, below_out_ref, 0), fields(below_mid_ref, below_out_ref, 2)
    gain_below = [h + r for h, r in zip(high, rest)]
    pri = fields(below_mid_ref, below_out_ref, 4)
    bwd = [p - g for p, g in zip(pri, gain_below)]
    high, rest = fields(before_mid_ref, before_out_ref, 0), fields(before_mid_ref, before_out_ref, 2)
    far = [jnp.where(depth_ref[0] > 1, h + r, 0.0) for h, r in zip(high, rest)]
    part_before = fields(before_mid_ref, before_out_ref, 4)
    part_above = fields(above_mid_ref, above_out_ref, 0)
    if not deep:
        high, rest = fields(above_mid_ref, above_out_ref, 2), fields(above_mid_ref, above_out_ref, 4)
        far = [f + jnp.where(depth_ref[0] > 2, h + r, 0.0) for f, h, r in zip(far, high, rest)]

    start = [0.5 * (f + g) for f, g in zip(far, gain_below)]
    start_up = [s + 0.5 * g for s, g in zip(start, gain)]
    start_down = [s - 0.5 * g for s, g in zip(start, gain_below)]
    part = pair_pull([0.5 * g for g in gain], here, fwd, ahd)
    part_below = pair_pull([0.5 * g for g in gain_below], below, pri, bwd)

    weights = springs_of(stiff, edges)
    first = eased(start, weights, inside, edges)
    first = [u + p - q for u, p, q in zip(first, part, part_below)]
    first_up = eased(start_up, springs_of(stiff_up, edges), inside_up, edges)
    first_up = [u + p - q for u, p, q in zip(first_up, part_above, part)]
    first_down = eased(start_down, springs_of(stiff_down, edges), inside_down, edges)
    first_down = [u + p - q for u, p, q in zip(first_down, part_below, part_before)]
    pull = pair_pull([a - b for a, b in zip(first_up, first)], here, fwd, ahd)
    push = pair_pull([a - b for a, b in zip(first, first_down)], below, pri, bwd)
    second = [
        u + p - q for u, p, q in zip(eased(first, weights, inside, edges), pull, push)
    ]
    for i in range(2):
        change_ref[i] = (second[i] - start[i])[FRAME : FRAME + height].astype(jnp.bfloat16)
    for i, value in enumerate([*second, *start_up, *start_down, *fwd, *ahd, *pri, *bwd, here, below, stiff]):
        state_ref[i] = value


def late_kernel(depth_ref, even_ref, odd_ref, state_ref, out_ref):
    rows, cols = state_ref.shape[1:]
    height = rows - 2 * FRAME
    body = slice(FRAME, FRAME + height)
    col = lax.broadcasted_iota(jnp.int32, (rows, cols), 1)
    edges = (col == 0, col == cols - 1)
    second = [state_ref[i] for i in range(2)]
    stiff = state_ref[16]
    third = eased(second, springs_of(stiff, edges), stiff > 0.0, edges)

    def two(at):
        return [state_ref[at + i, body, :] for i in range(2)]

    mid = two(0)
    first_of_pair = depth_ref[0] % 2 == 0
    swaps = [(even_ref[i].astype(jnp.float32), odd_ref[i].astype(jnp.float32)) for i in range(2)]
    up = [a + jnp.where(first_of_pair, e, o) - m for a, m, (e, o) in zip(two(2), mid, swaps)]
    down = [m - a - jnp.where(first_of_pair, o, e) for a, m, (e, o) in zip(two(4), mid, swaps)]
    pull = pair_pull(up, state_ref[14, body, :], two(6), two(8))
    push = pair_pull(down, state_ref[15, body, :], two(10), two(12))
    for i in range(2):
        out_ref[i] = third[i][body] + pull[i] - push[i]


def relaxation(change_shape, links, stiffness, depth, arrays):
    height, breadth = change_shape[1:]
    vmem, smem = pl.BlockSpec(memory_space=pltpu.VMEM), pl.BlockSpec(memory_space=pltpu.SMEM)
    change, state = pl.pallas_call(
        functools.partial(early_kernel, lax.axis_size("gz") > 4),
        out_shape=(
            jax.ShapeDtypeStruct(change_shape, jnp.bfloat16),
            jax.ShapeDtypeStruct((17, height + 2 * FRAME, breadth), jnp.float32),
        ),
        in_specs=[smem] * 3 + [vmem] * len(arrays),
        out_specs=(vmem, vmem),
        scratch_shapes=[pltpu.VMEM((height + 2 * FRAME, breadth), jnp.float32)],
        compiler_params=pltpu.CompilerParams(vmem_limit_bytes=16 * 2**20),
        cost_estimate=pl.CostEstimate(flops=2**23, bytes_accessed=2**21, transcendentals=2**16),
        name="early_steps",
    )(links, stiffness, depth, *arrays)
    even = swapped(change, "gz", 0)
    odd = swapped(change, "gz", 1)
    return pl.pallas_call(
        late_kernel,
        out_shape=jax.ShapeDtypeStruct(change_shape, jnp.float32),
        in_specs=[smem] + [vmem] * 3,
        out_specs=vmem,
        compiler_params=pltpu.CompilerParams(vmem_limit_bytes=16 * 2**20),
        cost_estimate=pl.CostEstimate(flops=2**22, bytes_accessed=2**21, transcendentals=2**15),
        name="last_step",
    )(depth, even, odd, state)


def whole_device(features, class_map, stiffness, valid):
    center = jnp.transpose(features[0], (1, 0, 2))
    height, channels, breadth = center.shape
    section, sections = lax.axis_index("gz"), lax.axis_size("gz")
    tile, tiles = lax.axis_index(tile_axes), lax.axis_size(tile_axes)
    quarter = height // 4
    low, high = quarter - RADIUS, height - quarter + RADIUS

    upper_mid = ringed(center[low:high], "gz", -1)

    codes = (class_map[0] + 1).astype(jnp.bfloat16).reshape(-1, channels, breadth)
    top = jnp.concatenate([center[:RADIUS], codes[:1]])
    bottom = jnp.concatenate([center[-RADIUS:], codes[-1:]])
    nothing = jnp.zeros_like(top)
    before = jnp.where(tile > 0, ringed(bottom, tile_axes, 1), nothing)
    after = jnp.where(tile < tiles - 1, ringed(top, tile_axes, -1), nothing)
    own_codes = jnp.concatenate(
        [before[RADIUS, -STEPS:], codes.reshape(height, breadth), after[RADIUS, :STEPS]]
    )
    spare = -own_codes.shape[0] % channels
    packed = jnp.pad(own_codes, ((0, spare), (0, 0))).reshape(-1, channels, breadth)
    upper_out = ringed(
        jnp.concatenate([before[:RADIUS], center[:low], center[high:], after[:RADIUS], packed]),
        "gz",
        -1,
    )
    outer = low + RADIUS
    upper_codes = upper_out[2 * outer :].reshape(-1, breadth)[: own_codes.shape[0]]

    def own_at(row):
        if row < 0:
            return 1, row + RADIUS
        return (0, row) if row < height else (2, row - height)

    def upper_at(row):
        if low <= row < high:
            return 0, row - low
        return (1, row + RADIUS) if row < low else (1, row - high + outer)

    sound = jnp.pad(valid.astype(jnp.float32), ((1, 1), (1, 1)))
    near = lax.dynamic_slice(sound, (section, tile), (3, 3))
    links = near[:-1] * near[1:]
    by_row = jnp.concatenate(
        [
            jnp.broadcast_to(links[:, k : k + 1], (2, count))
            for k, count in enumerate((STEPS, height, STEPS))
        ],
        axis=1,
    )

    def own_links(begin, count):
        return by_row[1][None, begin : begin + count, None]

    live = jnp.where(section < sections - 1, 1.0, 0.0)[None]
    middle_rows = range(quarter, height - quarter, BLOCK)
    middle = flows(live, [center], [upper_mid], own_at, upper_at, middle_rows)
    by_mid = own_links(quarter + STEPS, height // 2)
    sent_mid = messages(middle, by_mid, section)
    n_mid = 6 * middle.shape[1]
    below_mid = ringed(jnp.concatenate([sent_mid[0].reshape(n_mid, breadth), own_codes]), "gz", 1)
    before_mid = ringed(sent_mid[1], "gz", 2)
    above_mid = ringed(sent_mid[2], "gz", -1)
    outer_rows = [*range(0, quarter, BLOCK), *range(height - quarter, height, BLOCK)]
    outside = flows(
        live, [center, before, after], [upper_mid, upper_out], own_at, upper_at, outer_rows
    )

    head, tail = outside[:, :quarter], outside[:, quarter:]
    head = jnp.concatenate([ringed(tail[:, -STEPS:], tile_axes, 1), head], axis=1)
    tail = jnp.concatenate([tail, ringed(outside[:, :STEPS], tile_axes, -1)], axis=1)
    edge_rows = jnp.concatenate([head, tail], axis=1)
    first_tail = head.shape[1]
    by_edge = jnp.concatenate(
        [own_links(0, first_tail), own_links(height + 2 * STEPS - first_tail, first_tail)], axis=1
    )
    sent_out = messages(edge_rows, by_edge, section)
    below_out = ringed(sent_out[0], "gz", 1)
    before_out = ringed(sent_out[1], "gz", 2)
    above_out = ringed(sent_out[2], "gz", -1)

    forward = jnp.concatenate(
        [outside[:2, :quarter], middle[:2], outside[:2, quarter:]], axis=1
    )
    arrays = [
        middle,
        edge_rows,
        below_mid[:n_mid].reshape(6, -1, breadth),
        below_out,
        before_mid,
        before_out,
        above_mid,
        above_out,
        own_codes,
        upper_codes,
        below_mid[n_mid:],
    ]
    third = relaxation((2, height, breadth), links, stiffness, section[None], arrays)
    return (third[None], forward[None])


def solution(mesh):
    placed = (
        P(("groups", "gz"), None, tile_axes, None),
        P(("groups", "gz"), tile_axes, None),
        P(),
        P("groups", None),
    )
    return jax.shard_map(
        whole_device,
        mesh=mesh,
        in_specs=placed,
        out_specs=(P(("groups", "gz"), None, tile_axes, None),) * 2,
        check_vma=False,
    )
```
